256 devices in a mesh: band: 8 (over x_lo, y), dev: 32 (over x_hi, z, core).
Axes of the slice: x: 4 (x_hi: 2, x_lo: 2; x = x_hi * 2 + x_lo), y: 4, z: 8, core: 2. Of those that a mesh axis runs over, the one named last changes fastest.
Arguments:
- drive: float32 [2, 32, 131072], P(None, None, ('band', 'dev')), may hold values from -6 to 6
- coords: float32 [3, 131072], P(None, ('band', 'dev')), may hold values from 0 to 3
- rule_index: int32 [131072], P(('band', 'dev')), may hold values from 0 to 3
- rule_weight: float32 [4], replicated, may hold values from 0.1 to 0.4
- pair_cols: int32 [24576], P(('band', 'dev')), may hold values from 0 to 511, as said below
- pair_count: int32 [256], P(('band', 'dev')), may hold values from 12 to 96, as said below
Outputs:
- near_field: float32 [2, 32, 131072], P(None, None, ('band', 'dev'))
The draws below stay inside these ranges and needn't reach their ends.
Inputs may be any that keep to these rules, and one draw needn't show every extreme that they name: `pair_cols`: for slot s of device k the listed block column lies from k * 2 + (s mod 2) up to that row plus 64 - 1; slots s < 2 list the diagonal pair. `pair_count`: some device has all 96 slots live.
All inputs are finite; a program needn't handle non-finite values.
Results may differ from the reference program's by a relative error of at most 0.0003.
Values sent between devices are 32-bit elements; how exact they have to be, the bound alone decides.
A program may use at most 64 MiB of HBM per device.

```python
import math
import jax
import jax.numpy as jnp
from jax import lax

BLOCK = 256
NRHS = 32
RULES = 4
BR_DEV = 2
TILE_DEV = 96
NB = 512
BAND_ROWS = 64
UNKNOWNS = 131072


def draw_pair_cols(key, part):
    slot_ids = jnp.arange(NB // BR_DEV * TILE_DEV, dtype=jnp.int32)
    local_slot = slot_ids % TILE_DEV
    row_block = slot_ids // TILE_DEV * BR_DEV + local_slot % BR_DEV
    offsets = jax.random.randint(key, slot_ids.shape, 0, BAND_ROWS, dtype=jnp.int32)
    offsets = jnp.where(local_slot < BR_DEV, 0, offsets)
    return row_block + offsets % (NB - row_block)


def draw_pair_count(key, part):
    devices = NB // BR_DEV
    first_draw = jax.random.randint(jax.random.fold_in(key, 1), (devices,), TILE_DEV // 8, TILE_DEV + 1, dtype=jnp.int32)
    second_draw = jax.random.randint(jax.random.fold_in(key, 2), (devices,), TILE_DEV // 8, TILE_DEV + 1, dtype=jnp.int32)
    counts = jnp.minimum(first_draw, second_draw)
    chosen = jax.random.randint(jax.random.fold_in(key, 3), (), 0, devices, dtype=jnp.int32)
    device_ids = jnp.arange(devices, dtype=jnp.int32)
    counts = jnp.where(device_ids == chosen, TILE_DEV, counts)
    counts = jnp.where(device_ids == (chosen + 1) % devices, TILE_DEV // 8, counts)
    return counts


def with_ends(entries, key, low, largest):
    place = [jax.random.randint(jax.random.fold_in(key, axis), (), 0, length) for axis, length in enumerate(entries.shape)]
    main_axis = entries.shape.index(max(entries.shape))
    beside = place[:main_axis] + [(place[main_axis] + 1) % entries.shape[main_axis]] + place[main_axis + 1:]
    return entries.at[tuple(place)].set(low).at[tuple(beside)].set(largest)


def levels(key, shape, shards, low, top_value):
    factor_of, own = 1.0, jax.random.fold_in(key, 6)
    for axis_at, blocks in shards:
        heights = jnp.exp(jax.random.uniform(jax.random.fold_in(own, axis_at), (blocks,), jnp.float32, low / len(shards), top_value / len(shards)))
        factor_of = factor_of * jnp.repeat(heights, shape[axis_at] // blocks).reshape([-1 if axis == axis_at else 1 for axis in range(len(shape))])
    return factor_of


def noise(rng, dims, width, most, pieces=(), held_as=jnp.bfloat16):
    result = jax.random.normal(rng, dims, jnp.float32) * width
    if len(pieces) > 0:
        result = levels(rng, dims, pieces, -0.22, 0.18) * result
    return jnp.clip(result, min=-most, max=most).astype(held_as)


def setup_inputs(seed: int = 0) -> dict:
    arg_keys = jax.random.split(jax.random.key(seed), 7)
    drive = noise(arg_keys[0], (2, NRHS, UNKNOWNS), 1.0, 6.0, ((2, 256),), jnp.float32)
    coords = jnp.clip(3.0 * jax.random.uniform(arg_keys[1], (3, UNKNOWNS), jnp.float32) ** levels(arg_keys[1], (3, UNKNOWNS), ((1, 256),), -0.2, 0.2), 0.0, 3.0)
    rule_index = with_ends(jax.random.randint(arg_keys[2], (UNKNOWNS,), 0, RULES), jax.random.fold_in(arg_keys[2], 1), 0, RULES - 1).astype(jnp.int32)
    rule_weight = jnp.clip(jnp.exp(jax.random.uniform(arg_keys[3], (RULES,), jnp.float32, math.log(0.1), math.log(0.4))), 0.1, 0.4)
    pair_cols = draw_pair_cols(jax.random.fold_in(arg_keys[6], 71), 0)
    pair_count = draw_pair_count(jax.random.fold_in(arg_keys[6], 71), 0)
    return {"drive": drive, "coords": coords, "rule_index": rule_index, "rule_weight": rule_weight, "pair_cols": pair_cols, "pair_count": pair_count}


wave_number = 25.0
smoothing = 0.05
highest = lax.Precision.HIGHEST

def point_weights(rule_index, rule_weight):
    matches = rule_index[:, None] == jnp.arange(RULES, dtype=jnp.int32)[None, :]
    return lax.optimization_barrier(jnp.sum(jnp.where(matches, rule_weight[None, :], jnp.zeros_like(rule_weight)[None, :]), axis=1))

def assemble(near_points, far_points, near_w, far_w):
    offsets = near_points[:, :, None] - far_points[:, None, :]
    distance = jnp.sqrt(lax.optimization_barrier(jnp.sum(offsets * offsets, axis=0)) + smoothing * smoothing)
    strength = near_w[:, None] * far_w[None, :] / (4.0 * math.pi * distance)
    phases = wave_number * distance
    return (strength * jnp.cos(phases), strength * jnp.sin(phases))

def complex_apply(vectors, real_part, imag_part, patterns):
    stacked = vectors.reshape(2 * patterns, vectors.shape[2])
    real_prod = jnp.dot(stacked, real_part, precision=highest, preferred_element_type=jnp.float32)
    imag_prod = jnp.dot(stacked, imag_part, precision=highest, preferred_element_type=jnp.float32)
    return jnp.stack([real_prod[:patterns] - imag_prod[patterns:], real_prod[patterns:] + imag_prod[:patterns]])

def add_block(near_field, update_block, block_index):
    previous = lax.dynamic_slice_in_dim(near_field, block_index * BLOCK, BLOCK, 2)
    return lax.dynamic_update_slice_in_dim(near_field, previous + update_block, block_index * BLOCK, 2)

def reference(drive, coords, rule_index, rule_weight, pair_cols, pair_count):
    weights = point_weights(rule_index, rule_weight)
    patterns = drive.shape[1]
    slot_ids = jnp.arange(NB // BR_DEV * TILE_DEV, dtype=jnp.int32)
    owner_dev = slot_ids // TILE_DEV
    local_slot = slot_ids % TILE_DEV
    row_blocks = (owner_dev * BR_DEV + local_slot % BR_DEV).astype(jnp.int32)
    is_live = local_slot < pair_count[owner_dev]

    def one_tile(near_field, entry_item):
        row_block, col_block, alive = entry_item
        near_x = lax.dynamic_slice_in_dim(drive, row_block * BLOCK, BLOCK, 2)
        far_x = lax.dynamic_slice_in_dim(drive, col_block * BLOCK, BLOCK, 2)
        near_points = lax.dynamic_slice_in_dim(coords, row_block * BLOCK, BLOCK, 1)
        far_points = lax.dynamic_slice_in_dim(coords, col_block * BLOCK, BLOCK, 1)
        near_w = lax.dynamic_slice_in_dim(weights, row_block * BLOCK, BLOCK, 0)
        far_w = lax.dynamic_slice_in_dim(weights, col_block * BLOCK, BLOCK, 0)
        real_part, imag_part = assemble(near_points, far_points, near_w, far_w)
        keep_mask = jnp.where(alive, 1.0, 0.0).astype(drive.dtype)
        mirror = jnp.where(alive & (row_block != col_block), 1.0, 0.0).astype(drive.dtype)
        direct = complex_apply(far_x, real_part.T, imag_part.T, patterns) * keep_mask
        mirrored = complex_apply(near_x, real_part, imag_part, patterns) * mirror
        near_field = add_block(near_field, direct, row_block)
        near_field = add_block(near_field, mirrored, col_block)
        return (near_field, None)
    near_field, _ = lax.scan(one_tile, jnp.zeros_like(drive), (row_blocks, pair_cols.astype(jnp.int32), is_live))
    return near_field
```

```python
import math, functools
import jax, jax.numpy as jnp
from jax import lax
from jax.sharding import PartitionSpec as P
from jax.experimental import pallas as pl
from jax.experimental.pallas import tpu as pltpu

BLOCK=256
TURN = 25.0 / (2.0 * math.pi)
GAIN = 25.0 / (8.0 * math.pi**2)
SMOOTH2 = (0.05*TURN)**2
SIN = (4.4428829191996, -7.308245696145797, 3.6063544112192103, -0.8461128844269574, 0.10982698484738432)
COS = (1.4142134965645703, -6.978850988181998, 5.739461169540789, -1.8835629799935238, 0.3106981771853715)
ROWS = 32

def horner(z, c):
    v = c[-1]
    for k in c[-2::-1]:
        v = v * z + k
    return v

def split(v):
    hi = v.astype(jnp.bfloat16)
    return hi, (v - hi.astype(jnp.float32)).astype(jnp.bfloat16)

def build_tile(row, col, p_ref, q_ref, hi_ref, lo_ref):
    qx = q_ref[col, 0:1, :]
    qy = q_ref[col, 1:2, :]
    qz = q_ref[col, 2:3, :]
    for r in range(0, BLOCK, ROWS):
        px = p_ref[row, 0, r:r+ROWS, :]
        py = p_ref[row, 1, r:r+ROWS, :]
        pz = p_ref[row, 2, r:r+ROWS, :]
        px = jnp.concatenate([px, px], axis=1)
        py = jnp.concatenate([py, py], axis=1)
        pz = jnp.concatenate([pz, pz], axis=1)
        dx = px - qx
        dy = py - qy
        dz = pz - qz
        d2 = dx*dx + (dy*dy + (dz*dz + SMOOTH2))
        inv = lax.rsqrt(d2)
        turns = d2 * inv
        f = turns - jnp.round(turns)
        z = f * f
        s = f * horner(z, SIN)
        c = horner(z, COS)
        t = inv * s
        re = inv - t * s
        im = t * c
        rh, rl = split(re)
        ih, il = split(im)
        hi_ref[r:r+ROWS, 0:BLOCK] = rh
        hi_ref[r:r+ROWS, BLOCK:] = ih
        lo_ref[r:r+ROWS, 0:BLOCK] = rl
        lo_ref[r:r+ROWS, BLOCK:] = il

NT = (((1,), (1,)), ((), ()))
NN = (((1,), (0,)), ((), ()))

def dotf(a, b, dims):
    return lax.dot_general(a, b, dims, preferred_element_type=jnp.float32)

def apply_tile(row, col, md, mm, li_ref, lj_ref, hi_ref, lo_ref, yi_ref, yj_ref):
    a = dotf(lj_ref[col], hi_ref[...], NT)
    b = dotf(lj_ref[col, 0:64, :], lo_ref[...], NT)
    yi_ref[row] += md * (a[:64] + a[64:] + b)
    a = dotf(li_ref[row, :, 0:BLOCK], hi_ref[:, 0:BLOCK], NN) + dotf(li_ref[row, :, BLOCK:], hi_ref[:, BLOCK:], NN)
    b = dotf(li_ref[row, 0:64, 0:BLOCK], lo_ref[:, 0:BLOCK], NN) + dotf(li_ref[row, 0:64, BLOCK:], lo_ref[:, BLOCK:], NN)
    yj_ref[col] += mm * (a[:64] + a[64:] + b)

def fill_vectors(b_ref, n, l_ref):
    @pl.loop(0, n)
    def _(k):
        for h in range(2):
            cs = slice(h*BLOCK, (h+1)*BLOCK)
            x = b_ref[k, 0:64, cs] * (b_ref[k, 67:68, cs] * GAIN)
            hi, lo = split(x)
            l_ref[2*k+h, 0:64, 0:BLOCK] = hi
            l_ref[2*k+h, 64:128, 0:BLOCK] = lo
            l_ref[2*k+h, 0:32, BLOCK:] = -hi[32:]
            l_ref[2*k+h, 32:64, BLOCK:] = hi[:32]
            l_ref[2*k+h, 64:96, BLOCK:] = -lo[32:]
            l_ref[2*k+h, 96:128, BLOCK:] = lo[:32]

def compute_kernel(bi_ref, bj_ref, yi_ref, yj_ref,
                   li, lj, p, q, mv, ms, work, hi0, lo0, hi1, lo1, sem):
    ring, zpos, core = place()
    cols = bi_ref[:, 68, 0:128]
    count = bi_ref[:, 69, 0:1]
    lane = lax.broadcasted_iota(jnp.int32, (8, 128), 1)
    cols = jnp.where(lane.astype(jnp.float32) < count, cols, -2.0)
    lane1 = lax.broadcasted_iota(jnp.int32, (8, 128), 1)
    want = (ring + lane1 // 4) * 32 + zpos * 4 + lane1 % 4
    want = jnp.where(lane1 < 12, want, -1).astype(jnp.float32)
    for i in range(2):
        m = jnp.zeros((8, 128), jnp.int32)
        for s in range(i, 96, 2):
            m += jnp.where(jnp.broadcast_to(cols[:, s:s+1], (8, 128)) == want, 1, 0)
        mv[i*8:(i+1)*8, :] = m
    cp = pltpu.make_async_copy(mv, ms, sem)
    cp.start()
    yi_ref[...] = jnp.zeros_like(yi_ref)
    yj_ref[...] = jnp.zeros_like(yj_ref)
    fill_vectors(bi_ref, 8, li)
    fill_vectors(bj_ref, 6, lj)
    @pl.loop(0, 8)
    def _(k):
        t = (bi_ref[k, 64:72, :] * TURN).T
        for h in range(2):
            for d in range(3):
                p[2*k+h, d] = jnp.broadcast_to(t[h*BLOCK:(h+1)*BLOCK, d:d+1], (BLOCK, 128))
    @pl.loop(0, 6)
    def _(k):
        for h in range(2):
            q[2*k+h] = bj_ref[k, 64:72, h*BLOCK:(h+1)*BLOCK] * TURN
    cp.wait()
    def scan_row(rr, n):
        i = rr // 8; zi = rr % 8
        for j in range(12):
            m = ms[rr, j]
            same = jnp.logical_and(zi == zpos, core * 2 + i == j) if j < 4 else False
            work[n] = ((zi*2 + i) * 16 + j) * 256 + m * 2 + (jnp.where(same, 1, 0) if j < 4 else 0)
            n = n + jnp.where(m > 0, 1, 0)
        return n
    n = lax.fori_loop(0, 16, scan_row, jnp.int32(0))
    for e in range(3):
        work[n + e] = 0
    def unpack(t):
        w = work[t]
        row = w // 4096
        col = (w // 256) % 16
        m = (w // 2) % 128
        md = m.astype(jnp.float32)
        mm = jnp.where(w % 2 == 1, 0, m).astype(jnp.float32)
        return row, col, md, mm
    row, col, _, _ = unpack(0)
    build_tile(row, col, p, q, hi0, lo0)
    @pl.loop(0, (n + 1) // 2)
    def _(k):
        r0, c0, d0, m0 = unpack(2*k)
        r1, c1, d1, m1 = unpack(2*k+1)
        r2, c2, _, _ = unpack(2*k+2)
        build_tile(r1, c1, p, q, hi1, lo1)
        apply_tile(r0, c0, d0, m0, li, lj, hi0, lo0, yi_ref, yj_ref)
        build_tile(r2, c2, p, q, hi0, lo0)
        apply_tile(r1, c1, d1, m1, li, lj, hi1, lo1, yi_ref, yj_ref)

VM = pl.BlockSpec(memory_space=pltpu.VMEM)
RINGS = 16
RING_LEN = 8
RULES = 4
SLOTS = 96


def place():
    me = lax.axis_index("band") * 32 + lax.axis_index("dev")
    return me // 16, (me // 2) % 8, me % 2


def device(ring, z, core):
    k = (ring % RINGS) * 16 + (z % RING_LEN) * 2 + core
    return (k // 32, k % 32)


def remote(src, dst, ssem, rsem, target):
    return pltpu.make_async_remote_copy(
        src_ref=src, dst_ref=dst, send_sem=ssem, recv_sem=rsem,
        device_id=target, device_id_type=pl.DeviceIdType.MESH,
    )


def greet(ring, z, core):
    barrier = pltpu.get_barrier_semaphore()
    peers = [device(ring, z + 1, core), device(ring, z - 1, core), device(ring, z, 1 - core)]
    for d in (1, -1, 2, -2):
        for c in range(2):
            peers.append(device(ring + d, z, c))
    for peer in peers:
        pl.semaphore_signal(barrier, inc=1, device_id=peer, device_id_type=pl.DeviceIdType.MESH)
    pl.semaphore_wait(barrier, len(peers))


CUTS = ((0, 40), (40, 72))
HOPS = 4


def gather_kernel(b_ref, bi_ref, bj_ref, ring_send, ring_recv, side_send, side_recv, own_sem):
    ring, z, core = place()
    greet(ring, z, core)
    started = []

    def hop(way, h, ch):
        step = 1 - 2 * way
        owner = (z - step * h) % RING_LEN
        lo, hi = CUTS[ch]
        rows = pl.ds(lo, hi - lo)
        src = b_ref.at[rows] if h == 0 else bi_ref.at[owner, rows]
        cp = remote(src, bi_ref.at[owner, rows], ring_send.at[way, h, ch], ring_recv.at[way, h, ch],
                    device(ring, z + step, core))
        return cp

    def used(way, h, ch):
        return h < HOPS - 1 or ch == way

    for ch in range(2):
        for way in range(2):
            cp = hop(way, 0, ch)
            cp.start()
            started.append(cp)
    sides = [(1, 0), (1, 1), (2, 0), (2, 1)]
    for n, (d, c) in enumerate(sides):
        cp = remote(b_ref, bj_ref.at[d * 2 + core], side_send.at[n], side_recv.at[d * 2 + core],
                    device(ring - d, z, c))
        cp.start()
        started.append(cp)
    cp = remote(b_ref, bj_ref.at[core], side_send.at[4], side_recv.at[core], device(ring, z, 1 - core))
    cp.start()
    started.append(cp)
    mine = [pltpu.make_async_copy(b_ref, bi_ref.at[z], own_sem.at[0]),
            pltpu.make_async_copy(b_ref, bj_ref.at[core], own_sem.at[1])]
    for cp in mine:
        cp.start()
    for h in range(1, HOPS):
        for ch in range(2):
            for way in range(2):
                hop(way, h - 1, ch).wait_recv()
                if used(way, h, ch):
                    cp = hop(way, h, ch)
                    cp.start()
                    started.append(cp)
    for way in range(2):
        hop(way, HOPS - 1, way).wait_recv()
    for d in (1, 2):
        for c in range(2):
            remote(b_ref, bj_ref.at[d * 2 + c], side_send.at[0], side_recv.at[d * 2 + c],
                   device(ring, z, 1 - core)).wait_recv()
    remote(b_ref, bj_ref.at[1 - core], side_send.at[4], side_recv.at[1 - core],
           device(ring, z, 1 - core)).wait_recv()
    for cp in started:
        cp.wait_send()
    for cp in mine:
        cp.wait()


def gather(b):
    f = jnp.float32
    dma = pltpu.SemaphoreType.DMA
    return pl.pallas_call(
        gather_kernel,
        out_shape=(jax.ShapeDtypeStruct((8, 72, 512), f), jax.ShapeDtypeStruct((6, 72, 512), f)),
        in_specs=[VM], out_specs=(VM, VM),
        scratch_shapes=[dma((2, HOPS, 2)), dma((2, HOPS, 2)), dma((5,)), dma((6,)), dma((2,))],
        compiler_params=pltpu.CompilerParams(collective_id=0, has_side_effects=True, vmem_limit_bytes=16 << 20),
    )(b)


def compute(bi, bj):
    f = jnp.float32
    b = jnp.bfloat16
    return pl.pallas_call(
        compute_kernel,
        out_shape=(jax.ShapeDtypeStruct((16, 64, 256), f), jax.ShapeDtypeStruct((12, 64, 256), f)),
        in_specs=[VM] * 2, out_specs=(VM, VM),
        scratch_shapes=[pltpu.VMEM((16, 128, 512), b), pltpu.VMEM((12, 128, 512), b),
                        pltpu.VMEM((16, 3, 256, 128), f), pltpu.VMEM((12, 8, 256), f),
                        pltpu.VMEM((16, 128), jnp.int32), pltpu.SMEM((16, 128), jnp.int32),
                        pltpu.SMEM((256,), jnp.int32),
                        pltpu.VMEM((256, 512), b), pltpu.VMEM((256, 512), b),
                        pltpu.VMEM((256, 512), b), pltpu.VMEM((256, 512), b),
                        pltpu.SemaphoreType.DMA],
        compiler_params=pltpu.CompilerParams(vmem_limit_bytes=48 << 20),
    )(bi, bj)


def reduce_kernel(yi_ref, yj_ref, w_ref, out_ref, flow, side, ring_send, ring_recv, side_send, side_recv):
    ring, z, core = place()
    greet(ring, z, core)
    started = []

    def part(ref, first, ch):
        return ref.at[pl.ds(first, 2), pl.ds(32 * ch, 32)]

    def hop(way, h, ch, src):
        step = 1 - 2 * way
        cp = remote(src, part(flow.at[way, h], 0, ch), ring_send.at[way, h, ch], ring_recv.at[way, h, ch],
                    device(ring, z + step, core))
        return cp

    def target(way, h):
        return (z + (1 - 2 * way) * (HOPS - h)) % RING_LEN

    def launch(cp):
        cp.start()
        started.append(cp)

    for way in range(2):
        launch(hop(way, 0, way, part(yi_ref, 2 * target(way, 0), way)))
    for way in range(2):
        launch(hop(way, 1, 1 - way, part(yi_ref, 2 * target(way, 1), 1 - way)))
    n = 0
    for d in (1, 2):
        for c in range(2):
            launch(remote(yj_ref.at[pl.ds((d * 2 + c) * 2, 2)], side.at[(d - 1) * 2 + core], side_send.at[n],
                          side_recv.at[(d - 1) * 2 + core], device(ring + d, z, c)))
            n += 1
    launch(remote(yj_ref.at[pl.ds((1 - core) * 2, 2)], side.at[4], side_send.at[4], side_recv.at[4],
                  device(ring, z, 1 - core)))
    for h in range(1, HOPS):
        for k in range(2):
            for way in range(2):
                ch = way if k == 0 else 1 - way
                if k == 1 and h == 1:
                    continue
                here = part(flow.at[way, h - 1], 0, ch)
                hop(way, h - 1, ch, here).wait_recv()
                rows = slice(32 * ch, 32 * ch + 32)
                flow[way, h - 1, :, rows, :] += yi_ref[pl.ds(2 * target(way, h), 2), rows, :]
                launch(hop(way, h, ch, here))
    for way in range(2):
        for ch in range(2):
            hop(way, HOPS - 1, ch, part(flow.at[way, 0], 0, ch)).wait_recv()
    for s in range(5):
        remote(side.at[s], side.at[s], side_send.at[s], side_recv.at[s], device(ring, z, 1 - core)).wait_recv()
    for h in range(2):
        total = yi_ref[2 * z + h] + yj_ref[2 * core + h]
        total += side[0, h] + side[1, h] + (side[2, h] + side[3, h]) + side[4, h]
        total += flow[0, HOPS - 1, h] + flow[1, HOPS - 1, h]
        out_ref[:, h * BLOCK:(h + 1) * BLOCK] = total * w_ref[3:4, h * BLOCK:(h + 1) * BLOCK]
    for cp in started:
        cp.wait_send()


def reduce(yi, yj, aux):
    f = jnp.float32
    dma = pltpu.SemaphoreType.DMA
    return pl.pallas_call(
        reduce_kernel,
        out_shape=jax.ShapeDtypeStruct((64, 512), f),
        in_specs=[VM] * 3, out_specs=VM,
        scratch_shapes=[pltpu.VMEM((2, HOPS, 2, 64, 256), f), pltpu.VMEM((5, 2, 64, 256), f),
                        dma((2, HOPS, 2)), dma((2, HOPS, 2)), dma((5,)), dma((5,))],
        compiler_params=pltpu.CompilerParams(collective_id=1, has_side_effects=True, vmem_limit_bytes=16 << 20),
    )(yi, yj, aux)


def body(drive, coords, rule_index, rule_weight, pair_cols, pair_count):
    weights = jnp.zeros((512,), jnp.float32)
    for r in range(RULES):
        weights = jnp.where(rule_index == r, rule_weight[r], weights)
    cols = jnp.pad(pair_cols.astype(jnp.float32), (0, 512 - SLOTS))
    count = jnp.broadcast_to(pair_count.astype(jnp.float32), (512,))
    aux = jnp.concatenate([coords, jnp.stack([weights, cols, count, count, count])], axis=0)
    b = jnp.concatenate([drive.reshape(64, 512), aux], axis=0)
    bi, bj = gather(b)
    yi, yj = compute(bi, bj)
    return reduce(yi, yj, aux).reshape(2, 32, 512)


def solution(mesh):
    both = ("band", "dev")
    in_specs = (P(None, None, both), P(None, both), P(both), P(), P(both), P(both))
    return jax.shard_map(body, mesh=mesh, in_specs=in_specs, out_specs=P(None, None, both), check_vma=False)
```

```python
import math

import jax
import jax.numpy as jnp
from jax import lax
from jax.experimental import pallas as pl
from jax.experimental.pallas import tpu as pltpu
from jax.sharding import PartitionSpec as P

BLOCK = 256
RULES = 4
SLOTS = 96
RINGS = 16
RING_LEN = 8
HOPS = 4
ROWS = 32
PACK = 72
WAVES = 25.0 / (2.0 * math.pi)
GAIN = 25.0 / (8.0 * math.pi**2)
SMOOTH = (0.05 * WAVES) ** 2
SINE = (2.6417539924711972, -1.0863767471480779, 0.1340056362838771, -0.007739908243745813)
FULL = 2.0 * math.sqrt(2.0)
HALF = math.sqrt(2.0)

VM = pl.BlockSpec(memory_space=pltpu.VMEM)
SM = pl.BlockSpec(memory_space=pltpu.SMEM)
MESH = pl.DeviceIdType.MESH
NT = (((1,), (1,)), ((), ()))
NN = (((1,), (0,)), ((), ()))


def place():
    me = lax.axis_index("band") * 32 + lax.axis_index("dev")
    return me // 16, (me // 2) % 8, me % 2


def device(ring, z, core):
    k = (ring % RINGS) * 16 + (z % RING_LEN) * 2 + core
    return (k // 32, k % 32)


def remote(src, dst, ssem, rsem, target):
    return pltpu.make_async_remote_copy(
        src_ref=src, dst_ref=dst, send_sem=ssem, recv_sem=rsem, device_id=target, device_id_type=MESH
    )


def partners(ring, z, core):
    peers = [device(ring, z + 1, core), device(ring, z - 1, core), device(ring, z, 1 - core)]
    for d in (1, -1, 2, -2):
        for c in range(2):
            peers.append(device(ring + d, z, c))
    return peers


def split(v):
    hi = v.astype(jnp.bfloat16)
    return hi, (v - hi.astype(jnp.float32)).astype(jnp.bfloat16)


def fill_vectors(src, slot, l_ref):
    for h in range(2):
        hi, lo = split(src[0:64, h * BLOCK:(h + 1) * BLOCK])
        k = 2 * slot + h
        l_ref[k, 0:64, 0:BLOCK] = hi
        l_ref[k, 64:128, 0:BLOCK] = lo
        l_ref[k, 0:32, BLOCK:] = -hi[32:]
        l_ref[k, 32:64, BLOCK:] = hi[:32]
        l_ref[k, 64:96, BLOCK:] = -lo[32:]
        l_ref[k, 96:128, BLOCK:] = lo[:32]


CUTS = ((0, 40), (40, PACK))


def gather_kernel(x_ref, c_ref, rule_ref, rw_ref, cols_ref, count_ref,
                  li_ref, lj_ref, p_ref, q_ref, table_ref, w_ref,
                  b_ref, bi_ref, bj_ref, ring_send, ring_recv, side_send, side_recv):
    ring, z, core = place()
    barrier = pltpu.get_barrier_semaphore()
    peers = partners(ring, z, core)
    for peer in peers:
        pl.semaphore_signal(barrier, inc=1, device_id=peer, device_id_type=MESH)

    rule = rule_ref[...]
    w = jnp.zeros((1, 512), jnp.float32)
    for r in range(RULES):
        w = jnp.where(rule == r, rw_ref[r], w)
    w_ref[...] = jnp.broadcast_to(w, (8, 512))
    b_ref[0:64, :] = x_ref[...] * (w * GAIN)
    b_ref[64:67, :] = c_ref[...] * WAVES
    b_ref[67:72, :] = jnp.full((5, 512), -2.0, jnp.float32)
    slot = lax.broadcasted_iota(jnp.int32, (1, SLOTS), 1)
    b_ref[67:68, 0:SLOTS] = jnp.where(slot < count_ref[0], cols_ref[...], -2).astype(jnp.float32)
    table_ref[...] = jnp.zeros_like(table_ref)

    pl.semaphore_wait(barrier, len(peers))
    started = []

    def launch(cp):
        cp.start()
        started.append(cp)

    def owner_of(way, h):
        return (z - (1 - 2 * way) * h) % RING_LEN

    def hop(way, h, ch):
        owner = owner_of(way, h)
        rows = pl.ds(CUTS[ch][0], CUTS[ch][1] - CUTS[ch][0])
        src = b_ref.at[rows] if h == 0 else bi_ref.at[owner, rows]
        return remote(src, bi_ref.at[owner, rows], ring_send.at[way, h, ch], ring_recv.at[way, h, ch],
                      device(ring, z + 1 - 2 * way, core))

    for ch in range(2):
        for way in range(2):
            launch(hop(way, 0, ch))
    for n, (d, c) in enumerate(((1, 0), (1, 1), (2, 0), (2, 1))):
        launch(remote(b_ref, bj_ref.at[d * 2 + core], side_send.at[n],
                      side_recv.at[d * 2 + core], device(ring - d, z, c)))
    launch(remote(b_ref, bj_ref.at[core], side_send.at[4], side_recv.at[core],
                  device(ring, z, 1 - core)))

    lane = lax.broadcasted_iota(jnp.int32, (16, 128), 1)
    col = lax.broadcasted_iota(jnp.int32, (16, 128), 0)
    want = jnp.where(col < 12, (ring + col // 4) * 32 + z * 4 + col % 4, -1).astype(jnp.float32)

    def expand_i(src, k):
        fill_vectors(src, k, li_ref)
        t = src[64:72, :].T
        for h in range(2):
            for d in range(3):
                p_ref[2 * k + h, d] = jnp.broadcast_to(t[h * BLOCK:(h + 1) * BLOCK, d:d + 1], (BLOCK, 128))
        hit = jnp.where(jnp.broadcast_to(src[67:68, 0:128], (16, 128)) == want, 1.0, 0.0)
        for i in range(2):
            m = jnp.sum(jnp.where(lane % 2 == i, hit, 0.0), axis=1, keepdims=True)
            table_ref[...] += jnp.where(lane == 2 * k + i, m, 0.0).astype(jnp.int32)

    def expand_j(src, k):
        fill_vectors(src, k, lj_ref)
        for h in range(2):
            q_ref[2 * k + h] = src[64:72, h * BLOCK:(h + 1) * BLOCK]

    expand_i(b_ref, z)
    expand_j(b_ref, core)
    for h in range(1, HOPS):
        for ch in range(2):
            for way in range(2):
                hop(way, h - 1, ch).wait_recv()
                if h < HOPS - 1 or ch == way:
                    launch(hop(way, h, ch))
        for way in range(2):
            k = owner_of(way, h)
            expand_i(bi_ref.at[k], k)
        js = ((1 - core, 4),) if h == 1 else ((4, 0), (5, 0)) if h == 2 else ((2, 0), (3, 0))
        for k, n in js:
            remote(b_ref, bj_ref.at[k], side_send.at[n], side_recv.at[k],
                   device(ring, z, 1 - core)).wait_recv()
            expand_j(bj_ref.at[k], k)
    for way in range(2):
        hop(way, HOPS - 1, way).wait_recv()
    k = (z + HOPS) % RING_LEN
    expand_i(bi_ref.at[k], k)
    for cp in started:
        cp.wait_send()


def gather(x, coords, rule, rw, cols, count):
    f = jnp.float32
    b = jnp.bfloat16
    dma = pltpu.SemaphoreType.DMA
    s = jax.ShapeDtypeStruct
    return pl.pallas_call(
        gather_kernel,
        out_shape=(s((16, 128, 512), b), s((12, 128, 512), b), s((16, 3, 256, 128), f), s((12, 8, 256), f),
                   s((16, 128), jnp.int32), s((8, 512), f)),
        in_specs=[VM, VM, VM, SM, VM, SM],
        out_specs=(VM,) * 6,
        scratch_shapes=[pltpu.VMEM((PACK, 512), f), pltpu.VMEM((8, PACK, 512), f), pltpu.VMEM((6, PACK, 512), f),
                        dma((2, HOPS, 2)), dma((2, HOPS, 2)), dma((5,)), dma((6,))],
        compiler_params=pltpu.CompilerParams(collective_id=0, has_side_effects=True, vmem_limit_bytes=20 << 20),
    )(x, coords, rule, rw, cols, count)


def build_tile(row, col, p_ref, q_ref, hi_ref, lo_ref):
    qx = q_ref[col, 0:1, :]
    qy = q_ref[col, 1:2, :]
    qz = q_ref[col, 2:3, :]
    for r in range(0, BLOCK, ROWS):
        px = p_ref[row, 0, r:r + ROWS, :]
        py = p_ref[row, 1, r:r + ROWS, :]
        pz = p_ref[row, 2, r:r + ROWS, :]
        dx = jnp.concatenate([px, px], axis=1) - qx
        dy = jnp.concatenate([py, py], axis=1) - qy
        dz = jnp.concatenate([pz, pz], axis=1) - qz
        square = dx * dx + (dy * dy + (dz * dz + SMOOTH))
        inv = lax.rsqrt(square)
        turns = square * inv
        f = turns - jnp.round(turns)
        f2 = f * f
        poly = SINE[-1]
        for k in SINE[-2::-1]:
            poly = poly * f2 + k
        s = f * poly
        ss = s * s
        rest = FULL - ss
        sh = s * (rest * lax.rsqrt(rest))
        ch = HALF - ss
        t = inv * sh
        rh, rl = split(inv - t * sh)
        ih, il = split(t * ch)
        hi_ref[r:r + ROWS, 0:BLOCK] = rh
        hi_ref[r:r + ROWS, BLOCK:] = ih
        lo_ref[r:r + ROWS, 0:BLOCK] = rl
        lo_ref[r:r + ROWS, BLOCK:] = il


def dotf(a, b, dims):
    return lax.dot_general(a, b, dims, preferred_element_type=jnp.float32)


def apply_tile(row, col, md, mm, li_ref, lj_ref, hi_ref, lo_ref, yi_ref, yj_ref):
    a = dotf(lj_ref[col], hi_ref[...], NT)
    b = dotf(lj_ref[col, 0:64, :], lo_ref[...], NT)
    yi_ref[row] += md * (a[:64] + a[64:] + b)
    a = dotf(li_ref[row, :, 0:BLOCK], hi_ref[:, 0:BLOCK], NN) + dotf(li_ref[row, :, BLOCK:], hi_ref[:, BLOCK:], NN)
    b = dotf(li_ref[row, 0:64, 0:BLOCK], lo_ref[:, 0:BLOCK], NN) + dotf(
        li_ref[row, 0:64, BLOCK:], lo_ref[:, BLOCK:], NN)
    yj_ref[col] += mm * (a[:64] + a[64:] + b)


def compute_kernel(li, lj, p, q, table, yi_ref, yj_ref, counts, work, hi0, lo0, hi1, lo1, sem):
    _, z, core = place()
    cp = pltpu.make_async_copy(table, counts, sem)
    cp.start()
    yi_ref[...] = jnp.zeros_like(yi_ref)
    yj_ref[...] = jnp.zeros_like(yj_ref)
    cp.wait()

    def scan_row(row, n):
        for j in range(12):
            m = counts[j, row]
            code = row * 4096 + j * 256 + m * 2
            work[n] = code
            n = n + jnp.where(m > 0, 1, 0)
        return n

    n = lax.fori_loop(0, 16, scan_row, jnp.int32(0))
    for e in range(3):
        work[n + e] = 0

    def unpack(t):
        w = work[t]
        row = lax.shift_right_logical(w, 12)
        col = lax.shift_right_logical(w, 8) & 15
        m = lax.shift_right_logical(w, 1) & 127
        same = jnp.logical_and(lax.shift_right_logical(row, 1) == z, col == core * 2 + (row & 1))
        return row, col, m.astype(jnp.float32), jnp.where(same, 0, m).astype(jnp.float32)

    row, col, _, _ = unpack(0)
    build_tile(row, col, p, q, hi0, lo0)

    @pl.loop(0, (n + 1) // 2)
    def _(k):
        r0, c0, d0, m0 = unpack(2 * k)
        r1, c1, d1, m1 = unpack(2 * k + 1)
        r2, c2, _, _ = unpack(2 * k + 2)
        build_tile(r1, c1, p, q, hi1, lo1)
        apply_tile(r0, c0, d0, m0, li, lj, hi0, lo0, yi_ref, yj_ref)
        build_tile(r2, c2, p, q, hi0, lo0)
        apply_tile(r1, c1, d1, m1, li, lj, hi1, lo1, yi_ref, yj_ref)


def compute(li, lj, p, q, table):
    f = jnp.float32
    b = jnp.bfloat16
    return pl.pallas_call(
        compute_kernel,
        out_shape=(jax.ShapeDtypeStruct((16, 64, 256), f), jax.ShapeDtypeStruct((12, 64, 256), f)),
        in_specs=[VM] * 5, out_specs=(VM, VM),
        scratch_shapes=[pltpu.SMEM((16, 128), jnp.int32), pltpu.SMEM((256,), jnp.int32),
                        pltpu.VMEM((256, 512), b), pltpu.VMEM((256, 512), b),
                        pltpu.VMEM((256, 512), b), pltpu.VMEM((256, 512), b),
                        pltpu.SemaphoreType.DMA],
        compiler_params=pltpu.CompilerParams(vmem_limit_bytes=24 << 20),
    )(li, lj, p, q, table)


def reduce_kernel(yi_ref, yj_ref, w_ref, out_ref, flow, side, ring_send, ring_recv, side_send, side_recv):
    ring, z, core = place()
    barrier = pltpu.get_barrier_semaphore()
    peers = partners(ring, z, core)
    for peer in peers:
        pl.semaphore_signal(barrier, inc=1, device_id=peer, device_id_type=MESH)
    pl.semaphore_wait(barrier, len(peers))
    started = []

    def part(ref, first, ch):
        return ref.at[pl.ds(first, 2), pl.ds(32 * ch, 32)]

    def hop(way, h, ch, src):
        return remote(src, part(flow.at[way, h], 0, ch), ring_send.at[way, h, ch], ring_recv.at[way, h, ch],
                      device(ring, z + 1 - 2 * way, core))

    def target(way, h):
        return (z + (1 - 2 * way) * (HOPS - h)) % RING_LEN

    def launch(cp):
        cp.start()
        started.append(cp)

    for way in range(2):
        launch(hop(way, 0, way, part(yi_ref, 2 * target(way, 0), way)))
    for way in range(2):
        launch(hop(way, 1, 1 - way, part(yi_ref, 2 * target(way, 1), 1 - way)))
    n = 0
    for d in (1, 2):
        for c in range(2):
            launch(remote(yj_ref.at[pl.ds((d * 2 + c) * 2, 2)], side.at[(d - 1) * 2 + core], side_send.at[n],
                          side_recv.at[(d - 1) * 2 + core], device(ring + d, z, c)))
            n += 1
    launch(remote(yj_ref.at[pl.ds((1 - core) * 2, 2)], side.at[4], side_send.at[4], side_recv.at[4],
                  device(ring, z, 1 - core)))
    for h in range(1, HOPS):
        for k in range(2):
            for way in range(2):
                ch = way if k == 0 else 1 - way
                if k == 1 and h == 1:
                    continue
                here = part(flow.at[way, h - 1], 0, ch)
                hop(way, h - 1, ch, here).wait_recv()
                rows = slice(32 * ch, 32 * ch + 32)
                flow[way, h - 1, :, rows, :] += yi_ref[pl.ds(2 * target(way, h), 2), rows, :]
                launch(hop(way, h, ch, here))
    for way in range(2):
        for ch in range(2):
            hop(way, HOPS - 1, ch, part(flow.at[way, 0], 0, ch)).wait_recv()
    for s in range(5):
        remote(side.at[s], side.at[s], side_send.at[s], side_recv.at[s], device(ring, z, 1 - core)).wait_recv()
    for h in range(2):
        total = yi_ref[2 * z + h] + yj_ref[2 * core + h]
        total += side[0, h] + side[1, h] + (side[2, h] + side[3, h]) + side[4, h]
        total += flow[0, HOPS - 1, h] + flow[1, HOPS - 1, h]
        out_ref[:, h * BLOCK:(h + 1) * BLOCK] = total * w_ref[0:1, h * BLOCK:(h + 1) * BLOCK]
    for cp in started:
        cp.wait_send()


def reduce(yi, yj, w):
    f = jnp.float32
    dma = pltpu.SemaphoreType.DMA
    return pl.pallas_call(
        reduce_kernel,
        out_shape=jax.ShapeDtypeStruct((64, 512), f),
        in_specs=[VM] * 3, out_specs=VM,
        scratch_shapes=[pltpu.VMEM((2, HOPS, 2, 64, 256), f), pltpu.VMEM((5, 2, 64, 256), f),
                        dma((2, HOPS, 2)), dma((2, HOPS, 2)), dma((5,)), dma((5,))],
        compiler_params=pltpu.CompilerParams(collective_id=1, has_side_effects=True, vmem_limit_bytes=16 << 20),
    )(yi, yj, w)


def body(drive, coords, rule_index, rule_weight, pair_cols, pair_count):
    li, lj, p, q, table, w = gather(drive.reshape(64, 512), coords, rule_index.reshape(1, 512), rule_weight,
                                    pair_cols.reshape(1, SLOTS), pair_count)
    yi, yj = compute(li, lj, p, q, table)
    return reduce(yi, yj, w).reshape(2, 32, 512)


def solution(mesh):
    both = ("band", "dev")
    in_specs = (P(None, None, both), P(None, both), P(both), P(), P(both), P(both))
    return jax.shard_map(body, mesh=mesh, in_specs=in_specs, out_specs=P(None, None, both), check_vma=False)
```

```python
import math

import jax
import jax.numpy as jnp
from jax import lax
from jax.experimental import pallas as pl
from jax.experimental.pallas import tpu as pltpu
from jax.sharding import PartitionSpec as P

BLOCK = 256
RULES = 4
SLOTS = 96
RINGS = 16
RING_LEN = 8
HOPS = 4
ROWS = 32
PACK = 72
WAVES = 25.0 / (2.0 * math.pi)
GAIN = 25.0 / (8.0 * math.pi**2)
SMOOTH = (0.05 * WAVES) ** 2
SINE = (2.6417539924711972, -1.0863767471480779, 0.1340056362838771, -0.007739908243745813)
FULL = 2.0 * math.sqrt(2.0)
HALF = math.sqrt(2.0)

VM = pl.BlockSpec(memory_space=pltpu.VMEM)
HBM = pl.BlockSpec(memory_space=pltpu.HBM)
MESH = pl.DeviceIdType.MESH
NT = (((1,), (1,)), ((), ()))
NN = (((1,), (0,)), ((), ()))


def place():
    me = lax.axis_index("band") * 32 + lax.axis_index("dev")
    return me // 16, (me // 2) % 8, me % 2


def device(ring, z, core):
    k = (ring % RINGS) * 16 + (z % RING_LEN) * 2 + core
    return (k // 32, k % 32)


def remote(src, dst, ssem, rsem, target):
    return pltpu.make_async_remote_copy(
        src_ref=src, dst_ref=dst, send_sem=ssem, recv_sem=rsem, device_id=target, device_id_type=MESH
    )


def partners(ring, z, core):
    peers = [device(ring, z + 1, core), device(ring, z - 1, core), device(ring, z, 1 - core)]
    for d in (1, -1, 2, -2):
        for c in range(2):
            peers.append(device(ring + d, z, c))
    return peers


def split(v):
    hi = v.astype(jnp.bfloat16)
    return hi, (v - hi.astype(jnp.float32)).astype(jnp.bfloat16)


def fill_vectors(src, slot, l_ref):
    for h in range(2):
        hi, lo = split(src[0:64, h * BLOCK:(h + 1) * BLOCK])
        k = 2 * slot + h
        l_ref[k, 0:64, 0:BLOCK] = hi
        l_ref[k, 64:128, 0:BLOCK] = lo
        l_ref[k, 0:32, BLOCK:] = -hi[32:]
        l_ref[k, 32:64, BLOCK:] = hi[:32]
        l_ref[k, 64:96, BLOCK:] = -lo[32:]
        l_ref[k, 96:128, BLOCK:] = lo[:32]


def far(way, ch):
    return ch // (NCH // 2) == way


CUTS = (0, 40, 72)
NCH = len(CUTS) - 1


def gather_kernel(x_hbm, c_hbm, rule_hbm, rw_hbm, cols_hbm, count_ref,
                  li_ref, lj_ref, p_ref, q_ref, table_ref, w_ref,
                  b_ref, bi_ref, bj_ref, x_ref, c_ref, rule_ref, cols_ref, rw_ref,
                  ring_send, ring_recv, side_send, side_recv, load_sem):
    ring, z, core = place()
    loads = [pltpu.make_async_copy(src, dst, load_sem.at[n]) for n, (src, dst) in enumerate((
        (rule_hbm, rule_ref), (rw_hbm, rw_ref), (x_hbm, x_ref), (c_hbm, c_ref), (cols_hbm, cols_ref)))]
    for cp in loads:
        cp.start()
    barrier = pltpu.get_barrier_semaphore()
    peers = partners(ring, z, core)
    for peer in peers:
        pl.semaphore_signal(barrier, inc=1, device_id=peer, device_id_type=MESH)

    for cp in loads:
        cp.wait()
    rule = rule_ref[...]
    w = jnp.zeros((1, 512), jnp.float32)
    for r in range(RULES):
        w = jnp.where(rule == r, rw_ref[r], w)
    w_ref[...] = jnp.broadcast_to(w, (8, 512))
    b_ref[0:64, :] = x_ref[...] * (w * GAIN)
    b_ref[64:67, :] = c_ref[...] * WAVES
    b_ref[67:72, :] = jnp.full((5, 512), -2.0, jnp.float32)
    slot = lax.broadcasted_iota(jnp.int32, (1, SLOTS), 1)
    b_ref[67:68, 0:SLOTS] = jnp.where(slot < count_ref[0], cols_ref[...], -2).astype(jnp.float32)
    table_ref[...] = jnp.zeros_like(table_ref)

    pl.semaphore_wait(barrier, len(peers))
    started = []

    def launch(cp):
        cp.start()
        started.append(cp)

    def owner_of(way, h):
        return (z - (1 - 2 * way) * h) % RING_LEN

    def hop(way, h, ch):
        owner = owner_of(way, h)
        rows = pl.ds(CUTS[ch], CUTS[ch + 1] - CUTS[ch])
        src = b_ref.at[rows] if h == 0 else bi_ref.at[owner, rows]
        return remote(src, bi_ref.at[owner, rows], ring_send.at[way, h, ch], ring_recv.at[way, h, ch],
                      device(ring, z + 1 - 2 * way, core))

    for ch in range(NCH):
        for way in range(2):
            launch(hop(way, 0, ch))
    for n, (d, c) in enumerate(((1, 0), (1, 1), (2, 0), (2, 1))):
        launch(remote(b_ref, bj_ref.at[d * 2 + core], side_send.at[n],
                      side_recv.at[d * 2 + core], device(ring - d, z, c)))
    launch(remote(b_ref, bj_ref.at[core], side_send.at[4], side_recv.at[core],
                  device(ring, z, 1 - core)))

    lane = lax.broadcasted_iota(jnp.int32, (16, 128), 1)
    col = lax.broadcasted_iota(jnp.int32, (16, 128), 0)
    want = jnp.where(col < 12, (ring + col // 4) * 32 + z * 4 + col % 4, -1).astype(jnp.float32)

    def expand_i(src, k):
        fill_vectors(src, k, li_ref)
        t = src[64:72, :].T
        for h in range(2):
            for d in range(3):
                p_ref[2 * k + h, d] = jnp.broadcast_to(t[h * BLOCK:(h + 1) * BLOCK, d:d + 1], (BLOCK, 128))
        hit = jnp.where(jnp.broadcast_to(src[67:68, 0:128], (16, 128)) == want, 1.0, 0.0)
        for i in range(2):
            m = jnp.sum(jnp.where(lane % 2 == i, hit, 0.0), axis=1, keepdims=True)
            table_ref[...] += jnp.where(lane == 2 * k + i, m, 0.0).astype(jnp.int32)

    def expand_j(src, k):
        fill_vectors(src, k, lj_ref)
        for h in range(2):
            q_ref[2 * k + h] = src[64:72, h * BLOCK:(h + 1) * BLOCK]

    expand_i(b_ref, z)
    expand_j(b_ref, core)
    for h in range(1, HOPS):
        for ch in range(NCH):
            for way in range(2):
                hop(way, h - 1, ch).wait_recv()
                if h < HOPS - 1 or far(way, ch):
                    launch(hop(way, h, ch))
        for way in range(2):
            k = owner_of(way, h)
            expand_i(bi_ref.at[k], k)
        js = ((1 - core, 4),) if h == 1 else ((4, 0), (5, 0)) if h == 2 else ((2, 0), (3, 0))
        for k, n in js:
            remote(b_ref, bj_ref.at[k], side_send.at[n], side_recv.at[k],
                   device(ring, z, 1 - core)).wait_recv()
            expand_j(bj_ref.at[k], k)
    for way in range(2):
        for ch in range(NCH):
            if far(way, ch):
                hop(way, HOPS - 1, ch).wait_recv()
    k = (z + HOPS) % RING_LEN
    expand_i(bi_ref.at[k], k)
    for cp in started:
        cp.wait_send()


def gather(x, coords, rule, rw, cols, count):
    f = jnp.float32
    b = jnp.bfloat16
    dma = pltpu.SemaphoreType.DMA
    s = jax.ShapeDtypeStruct
    return pl.pallas_call(
        gather_kernel,
        out_shape=(s((16, 128, 512), b), s((12, 128, 512), b), s((16, 3, 256, 128), f), s((12, 8, 256), f),
                   s((16, 128), jnp.int32), s((8, 512), f)),
        in_specs=[HBM] * 5 + [pl.BlockSpec(memory_space=pltpu.SMEM)],
        out_specs=(VM,) * 6,
        scratch_shapes=[pltpu.VMEM((PACK, 512), f), pltpu.VMEM((8, PACK, 512), f), pltpu.VMEM((6, PACK, 512), f),
                        pltpu.VMEM((64, 512), f), pltpu.VMEM((3, 512), f), pltpu.VMEM((1, 512), jnp.int32),
                        pltpu.VMEM((1, SLOTS), jnp.int32), pltpu.SMEM((RULES,), f),
                        dma((2, HOPS, NCH)), dma((2, HOPS, NCH)), dma((5,)), dma((6,)), dma((5,))],
        compiler_params=pltpu.CompilerParams(collective_id=0, has_side_effects=True, vmem_limit_bytes=20 << 20),
    )(x, coords, rule, rw, cols, count)


def build_tile(row, col, p_ref, q_ref, hi_ref, lo_ref):
    qx = q_ref[col, 0:1, :]
    qy = q_ref[col, 1:2, :]
    qz = q_ref[col, 2:3, :]
    for r in range(0, BLOCK, ROWS):
        px = p_ref[row, 0, r:r + ROWS, :]
        py = p_ref[row, 1, r:r + ROWS, :]
        pz = p_ref[row, 2, r:r + ROWS, :]
        dx = jnp.concatenate([px, px], axis=1) - qx
        dy = jnp.concatenate([py, py], axis=1) - qy
        dz = jnp.concatenate([pz, pz], axis=1) - qz
        square = dx * dx + (dy * dy + (dz * dz + SMOOTH))
        inv = lax.rsqrt(square)
        turns = square * inv
        f = turns - jnp.round(turns)
        f2 = f * f
        poly = SINE[-1]
        for k in SINE[-2::-1]:
            poly = poly * f2 + k
        s = f * poly
        ss = s * s
        rest = FULL - ss
        sh = s * (rest * lax.rsqrt(rest))
        ch = HALF - ss
        t = inv * sh
        rh, rl = split(inv - t * sh)
        ih, il = split(t * ch)
        hi_ref[r:r + ROWS, 0:BLOCK] = rh
        hi_ref[r:r + ROWS, BLOCK:] = ih
        lo_ref[r:r + ROWS, 0:BLOCK] = rl
        lo_ref[r:r + ROWS, BLOCK:] = il


def dotf(a, b, dims):
    return lax.dot_general(a, b, dims, preferred_element_type=jnp.float32)


def apply_tile(row, col, md, mm, li_ref, lj_ref, hi_ref, lo_ref, yi_ref, yj_ref):
    a = dotf(lj_ref[col], hi_ref[...], NT)
    b = dotf(lj_ref[col, 0:64, :], lo_ref[...], NT)
    yi_ref[row] += md * (a[:64] + a[64:] + b)
    a = dotf(li_ref[row, :, 0:BLOCK], hi_ref[:, 0:BLOCK], NN) + dotf(li_ref[row, :, BLOCK:], hi_ref[:, BLOCK:], NN)
    b = dotf(li_ref[row, 0:64, 0:BLOCK], lo_ref[:, 0:BLOCK], NN) + dotf(
        li_ref[row, 0:64, BLOCK:], lo_ref[:, BLOCK:], NN)
    yj_ref[col] += mm * (a[:64] + a[64:] + b)


def compute_kernel(li, lj, p, q, table, yi_ref, yj_ref, counts, work, hi0, lo0, hi1, lo1, sem):
    _, z, core = place()
    cp = pltpu.make_async_copy(table, counts, sem)
    cp.start()
    yi_ref[...] = jnp.zeros_like(yi_ref)
    yj_ref[...] = jnp.zeros_like(yj_ref)
    cp.wait()

    def scan_row(row, n):
        for j in range(12):
            m = counts[j, row]
            code = row * 4096 + j * 256 + m * 2
            work[n] = code
            n = n + jnp.where(m > 0, 1, 0)
        return n

    n = lax.fori_loop(0, 16, scan_row, jnp.int32(0))
    for e in range(3):
        work[n + e] = 0

    def unpack(t):
        w = work[t]
        row = lax.shift_right_logical(w, 12)
        col = lax.shift_right_logical(w, 8) & 15
        m = lax.shift_right_logical(w, 1) & 127
        same = jnp.logical_and(lax.shift_right_logical(row, 1) == z, col == core * 2 + (row & 1))
        return row, col, m.astype(jnp.float32), jnp.where(same, 0, m).astype(jnp.float32)

    row, col, _, _ = unpack(0)
    build_tile(row, col, p, q, hi0, lo0)

    @pl.loop(0, (n + 1) // 2)
    def _(k):
        r0, c0, d0, m0 = unpack(2 * k)
        r1, c1, d1, m1 = unpack(2 * k + 1)
        r2, c2, _, _ = unpack(2 * k + 2)
        build_tile(r1, c1, p, q, hi1, lo1)
        apply_tile(r0, c0, d0, m0, li, lj, hi0, lo0, yi_ref, yj_ref)
        build_tile(r2, c2, p, q, hi0, lo0)
        apply_tile(r1, c1, d1, m1, li, lj, hi1, lo1, yi_ref, yj_ref)


def compute(li, lj, p, q, table):
    f = jnp.float32
    b = jnp.bfloat16
    return pl.pallas_call(
        compute_kernel,
        out_shape=(jax.ShapeDtypeStruct((16, 64, 256), f), jax.ShapeDtypeStruct((12, 64, 256), f)),
        in_specs=[VM] * 5, out_specs=(VM, VM),
        scratch_shapes=[pltpu.SMEM((16, 128), jnp.int32), pltpu.SMEM((256,), jnp.int32),
                        pltpu.VMEM((256, 512), b), pltpu.VMEM((256, 512), b),
                        pltpu.VMEM((256, 512), b), pltpu.VMEM((256, 512), b),
                        pltpu.SemaphoreType.DMA],
        compiler_params=pltpu.CompilerParams(vmem_limit_bytes=24 << 20),
    )(li, lj, p, q, table)


PARTS = 4
SPAN = 64 // PARTS


def near(way, ch):
    return ch // (PARTS // 2) == way


def reduce_kernel(yi_ref, yj_ref, w_ref, out_ref, flow, side, ring_send, ring_recv, side_send, side_recv):
    ring, z, core = place()
    barrier = pltpu.get_barrier_semaphore()
    peers = partners(ring, z, core)
    for peer in peers:
        pl.semaphore_signal(barrier, inc=1, device_id=peer, device_id_type=MESH)
    pl.semaphore_wait(barrier, len(peers))
    started = []

    def part(ref, first, ch):
        return ref.at[pl.ds(first, 2), pl.ds(SPAN * ch, SPAN)]

    def hop(way, h, ch, src):
        return remote(src, part(flow.at[way, h], 0, ch), ring_send.at[way, h, ch], ring_recv.at[way, h, ch],
                      device(ring, z + 1 - 2 * way, core))

    def target(way, h):
        return (z + (1 - 2 * way) * (HOPS - h)) % RING_LEN

    def launch(cp):
        cp.start()
        started.append(cp)

    for ch in range(PARTS):
        for way in range(2):
            if near(way, ch):
                launch(hop(way, 0, ch, part(yi_ref, 2 * target(way, 0), ch)))
    for ch in range(PARTS):
        for way in range(2):
            if not near(way, ch):
                launch(hop(way, 1, ch, part(yi_ref, 2 * target(way, 1), ch)))
    n = 0
    for d in (1, 2):
        for c in range(2):
            launch(remote(yj_ref.at[pl.ds((d * 2 + c) * 2, 2)], side.at[(d - 1) * 2 + core], side_send.at[n],
                          side_recv.at[(d - 1) * 2 + core], device(ring + d, z, c)))
            n += 1
    launch(remote(yj_ref.at[pl.ds((1 - core) * 2, 2)], side.at[4], side_send.at[4], side_recv.at[4],
                  device(ring, z, 1 - core)))
    for h in range(1, HOPS):
        for first in (False, True):
            for ch in range(PARTS):
                for way in range(2):
                    if near(way, ch) != first or (h == 1 and not first):
                        continue
                    here = part(flow.at[way, h - 1], 0, ch)
                    hop(way, h - 1, ch, here).wait_recv()
                    rows = slice(SPAN * ch, SPAN * ch + SPAN)
                    flow[way, h - 1, :, rows, :] += yi_ref[pl.ds(2 * target(way, h), 2), rows, :]
                    launch(hop(way, h, ch, here))
    for way in range(2):
        for ch in range(PARTS):
            hop(way, HOPS - 1, ch, part(flow.at[way, 0], 0, ch)).wait_recv()
    for s in range(5):
        remote(side.at[s], side.at[s], side_send.at[s], side_recv.at[s], device(ring, z, 1 - core)).wait_recv()
    for h in range(2):
        total = yi_ref[2 * z + h] + yj_ref[2 * core + h]
        total += side[0, h] + side[1, h] + (side[2, h] + side[3, h]) + side[4, h]
        total += flow[0, HOPS - 1, h] + flow[1, HOPS - 1, h]
        out_ref[:, h * BLOCK:(h + 1) * BLOCK] = total * w_ref[0:1, h * BLOCK:(h + 1) * BLOCK]
    for cp in started:
        cp.wait_send()


def reduce(yi, yj, w):
    f = jnp.float32
    dma = pltpu.SemaphoreType.DMA
    return pl.pallas_call(
        reduce_kernel,
        out_shape=jax.ShapeDtypeStruct((64, 512), f),
        in_specs=[VM] * 3, out_specs=VM,
        scratch_shapes=[pltpu.VMEM((2, HOPS, 2, 64, 256), f), pltpu.VMEM((5, 2, 64, 256), f),
                        dma((2, HOPS, PARTS)), dma((2, HOPS, PARTS)), dma((5,)), dma((5,))],
        compiler_params=pltpu.CompilerParams(collective_id=1, has_side_effects=True, vmem_limit_bytes=16 << 20),
    )(yi, yj, w)


def body(drive, coords, rule_index, rule_weight, pair_cols, pair_count):
    held = [pltpu.with_memory_space_constraint(v, pltpu.HBM) for v in (
        drive.reshape(64, 512), coords, rule_index.reshape(1, 512), rule_weight, pair_cols.reshape(1, SLOTS))]
    li, lj, p, q, table, w = gather(*held, pair_count)
    yi, yj = compute(li, lj, p, q, table)
    return reduce(yi, yj, w).reshape(2, 32, 512)


def solution(mesh):
    both = ("band", "dev")
    in_specs = (P(None, None, both), P(None, both), P(both), P(), P(both), P(both))
    return jax.shard_map(body, mesh=mesh, in_specs=in_specs, out_specs=P(None, None, both), check_vma=False)
```

```python
import math

import jax
import jax.numpy as jnp
from jax import lax
from jax.experimental import pallas as pl
from jax.experimental.pallas import tpu as pltpu
from jax.sharding import PartitionSpec as P

BLOCK = 256
RULES = 4
SLOTS = 96
RINGS = 16
RING_LEN = 8
HOPS = 4
ROWS = 32
PACK = 72
WAVES = 25.0 / (2.0 * math.pi)
GAIN = 25.0 / (8.0 * math.pi**2)
SMOOTH = (0.05 * WAVES) ** 2
SINE = (2.6417539924711972, -1.0863767471480779, 0.1340056362838771, -0.007739908243745813)
FULL = 2.0 * math.sqrt(2.0)
HALF = math.sqrt(2.0)

VM = pl.BlockSpec(memory_space=pltpu.VMEM)
HBM = pl.BlockSpec(memory_space=pltpu.HBM)
MESH = pl.DeviceIdType.MESH
NT = (((1,), (1,)), ((), ()))
NN = (((1,), (0,)), ((), ()))


def place():
    me = lax.axis_index("band") * 32 + lax.axis_index("dev")
    return me // 16, (me // 2) % 8, me % 2


def device(ring, z, core):
    k = (ring % RINGS) * 16 + (z % RING_LEN) * 2 + core
    return (k // 32, k % 32)


def remote(src, dst, ssem, rsem, target):
    return pltpu.make_async_remote_copy(
        src_ref=src, dst_ref=dst, send_sem=ssem, recv_sem=rsem, device_id=target, device_id_type=MESH
    )


def partners(ring, z, core):
    peers = [device(ring, z + 1, core), device(ring, z - 1, core), device(ring, z, 1 - core)]
    for d in (1, -1, 2, -2):
        for c in range(2):
            peers.append(device(ring + d, z, c))
    return peers


def split(v):
    hi = v.astype(jnp.bfloat16)
    return hi, (v - hi.astype(jnp.float32)).astype(jnp.bfloat16)


def fill_vectors(src, slot, l_ref):
    for h in range(2):
        hi, lo = split(src[0:64, h * BLOCK:(h + 1) * BLOCK])
        k = 2 * slot + h
        l_ref[k, 0:64, 0:BLOCK] = hi
        l_ref[k, 64:128, 0:BLOCK] = lo
        l_ref[k, 0:32, BLOCK:] = -hi[32:]
        l_ref[k, 32:64, BLOCK:] = hi[:32]
        l_ref[k, 64:96, BLOCK:] = -lo[32:]
        l_ref[k, 96:128, BLOCK:] = lo[:32]


def far(way, ch):
    return ch // (NCH // 2) == way


CUTS = (0, 40, 72)
NCH = len(CUTS) - 1


def gather_kernel(x_hbm, c_hbm, rule_hbm, rw_hbm, cols_hbm, count_ref,
                  li_ref, lj_ref, p_ref, q_ref, table_ref, other_ref, w_ref,
                  b_ref, bi_ref, bj_ref, x_ref, c_ref, rule_ref, cols_ref, rw_ref,
                  seen_ref, ring_send, ring_recv, side_send, side_recv, load_sem, seen_sem):
    ring, z, core = place()
    loads = [pltpu.make_async_copy(src, dst, load_sem.at[n]) for n, (src, dst) in enumerate((
        (rule_hbm, rule_ref), (rw_hbm, rw_ref), (x_hbm, x_ref), (c_hbm, c_ref), (cols_hbm, cols_ref)))]
    for cp in loads:
        cp.start()
    barrier = pltpu.get_barrier_semaphore()
    peers = partners(ring, z, core)
    for peer in peers:
        pl.semaphore_signal(barrier, inc=1, device_id=peer, device_id_type=MESH)

    for cp in loads:
        cp.wait()
    rule = rule_ref[...]
    w = jnp.zeros((1, 512), jnp.float32)
    for r in range(RULES):
        w = jnp.where(rule == r, rw_ref[r], w)
    w_ref[...] = jnp.broadcast_to(w, (8, 512))
    b_ref[0:64, :] = x_ref[...] * (w * GAIN)
    b_ref[64:67, :] = c_ref[...] * WAVES
    b_ref[67:72, :] = jnp.full((5, 512), -2.0, jnp.float32)
    slot = lax.broadcasted_iota(jnp.int32, (1, SLOTS), 1)
    b_ref[67:68, 0:SLOTS] = jnp.where(slot < count_ref[0], cols_ref[...], -2).astype(jnp.float32)
    table_ref[...] = jnp.zeros_like(table_ref)

    pl.semaphore_wait(barrier, len(peers))
    started = []

    def launch(cp):
        cp.start()
        started.append(cp)

    def owner_of(way, h):
        return (z - (1 - 2 * way) * h) % RING_LEN

    def hop(way, h, ch):
        owner = owner_of(way, h)
        rows = pl.ds(CUTS[ch], CUTS[ch + 1] - CUTS[ch])
        src = b_ref.at[rows] if h == 0 else bi_ref.at[owner, rows]
        return remote(src, bi_ref.at[owner, rows], ring_send.at[way, h, ch], ring_recv.at[way, h, ch],
                      device(ring, z + 1 - 2 * way, core))

    for ch in range(NCH):
        for way in range(2):
            launch(hop(way, 0, ch))
    for n, (d, c) in enumerate(((1, 0), (1, 1), (2, 0), (2, 1))):
        launch(remote(b_ref, bj_ref.at[d * 2 + core], side_send.at[n],
                      side_recv.at[d * 2 + core], device(ring - d, z, c)))
    launch(remote(b_ref, bj_ref.at[core], side_send.at[4], side_recv.at[core],
                  device(ring, z, 1 - core)))

    lane = lax.broadcasted_iota(jnp.int32, (16, 128), 1)
    col = lax.broadcasted_iota(jnp.int32, (16, 128), 0)
    want = jnp.where(col < 12, (ring + col // 4) * 32 + z * 4 + col % 4, -1).astype(jnp.float32)

    def expand_i(src, k, listed=True):
        fill_vectors(src, k, li_ref)
        t = src[64:72, :].T
        for h in range(2):
            for d in range(3):
                p_ref[2 * k + h, d] = jnp.broadcast_to(t[h * BLOCK:(h + 1) * BLOCK, d:d + 1], (BLOCK, 128))
        if not listed:
            return
        hit = jnp.where(jnp.broadcast_to(src[67:68, 0:128], (16, 128)) == want, 1.0, 0.0)
        for i in range(2):
            m = jnp.sum(jnp.where(lane % 2 == i, hit, 0.0), axis=1, keepdims=True)
            table_ref[...] += jnp.where(lane == 2 * k + i, m, 0.0).astype(jnp.int32)

    def expand_j(src, k):
        fill_vectors(src, k, lj_ref)
        for h in range(2):
            q_ref[2 * k + h] = src[64:72, h * BLOCK:(h + 1) * BLOCK]

    expand_i(b_ref, z)
    expand_j(b_ref, core)
    for h in range(1, HOPS):
        for ch in range(NCH):
            for way in range(2):
                hop(way, h - 1, ch).wait_recv()
                if h < HOPS - 1 or far(way, ch):
                    launch(hop(way, h, ch))
        for way in range(2):
            k = owner_of(way, h)
            expand_i(bi_ref.at[k], k)
        js = ((1 - core, 4),) if h == 1 else ((4, 0), (5, 0)) if h == 2 else ((2, 0), (3, 0))
        for k, n in js:
            remote(b_ref, bj_ref.at[k], side_send.at[n], side_recv.at[k],
                   device(ring, z, 1 - core)).wait_recv()
            expand_j(bj_ref.at[k], k)
            if n == 4:
                expand_i(bj_ref.at[k], RING_LEN, listed=False)
        if h == HOPS - 1:
            have = table_ref[...]
            tally = jnp.sum(jnp.where(have > 0, 1.0, 0.0)).astype(jnp.int32)
            have = jnp.where(col == 15, tally, have)
            seen_ref[...] = have
            table_ref[...] = have
    note = remote(seen_ref, other_ref, seen_sem.at[0], seen_sem.at[1], device(ring, z, 1 - core))
    note.start()
    for way in range(2):
        for ch in range(NCH):
            if far(way, ch):
                hop(way, HOPS - 1, ch).wait_recv()
    k = (z + HOPS) % RING_LEN
    expand_i(bi_ref.at[k], k)
    note.wait()
    for cp in started:
        cp.wait_send()


def gather(x, coords, rule, rw, cols, count):
    f = jnp.float32
    b = jnp.bfloat16
    dma = pltpu.SemaphoreType.DMA
    s = jax.ShapeDtypeStruct
    return pl.pallas_call(
        gather_kernel,
        out_shape=(s((18, 128, 512), b), s((12, 128, 512), b), s((18, 3, 256, 128), f), s((12, 8, 256), f),
                   s((16, 128), jnp.int32), s((16, 128), jnp.int32), s((8, 512), f)),
        in_specs=[HBM] * 5 + [pl.BlockSpec(memory_space=pltpu.SMEM)],
        out_specs=(VM,) * 7,
        scratch_shapes=[pltpu.VMEM((PACK, 512), f), pltpu.VMEM((8, PACK, 512), f), pltpu.VMEM((6, PACK, 512), f),
                        pltpu.VMEM((64, 512), f), pltpu.VMEM((3, 512), f), pltpu.VMEM((1, 512), jnp.int32),
                        pltpu.VMEM((1, SLOTS), jnp.int32), pltpu.SMEM((RULES,), f), pltpu.VMEM((16, 128), jnp.int32),
                        dma((2, HOPS, NCH)), dma((2, HOPS, NCH)), dma((5,)), dma((6,)), dma((5,)), dma((2,))],
        compiler_params=pltpu.CompilerParams(collective_id=0, has_side_effects=True, vmem_limit_bytes=20 << 20),
    )(x, coords, rule, rw, cols, count)


def build_tile(row, col, p_ref, q_ref, hi_ref, lo_ref):
    qx = q_ref[col, 0:1, :]
    qy = q_ref[col, 1:2, :]
    qz = q_ref[col, 2:3, :]
    for r in range(0, BLOCK, ROWS):
        px = p_ref[row, 0, r:r + ROWS, :]
        py = p_ref[row, 1, r:r + ROWS, :]
        pz = p_ref[row, 2, r:r + ROWS, :]
        dx = jnp.concatenate([px, px], axis=1) - qx
        dy = jnp.concatenate([py, py], axis=1) - qy
        dz = jnp.concatenate([pz, pz], axis=1) - qz
        square = dx * dx + (dy * dy + (dz * dz + SMOOTH))
        inv = lax.rsqrt(square)
        turns = square * inv
        f = turns - jnp.round(turns)
        f2 = f * f
        poly = SINE[-1]
        for k in SINE[-2::-1]:
            poly = poly * f2 + k
        s = f * poly
        ss = s * s
        rest = FULL - ss
        sh = s * (rest * lax.rsqrt(rest))
        ch = HALF - ss
        t = inv * sh
        rh, rl = split(inv - t * sh)
        ih, il = split(t * ch)
        hi_ref[r:r + ROWS, 0:BLOCK] = rh
        hi_ref[r:r + ROWS, BLOCK:] = ih
        lo_ref[r:r + ROWS, 0:BLOCK] = rl
        lo_ref[r:r + ROWS, BLOCK:] = il


def dotf(a, b, dims):
    return lax.dot_general(a, b, dims, preferred_element_type=jnp.float32)


def apply_tile(row, col, md, mm, li_ref, lj_ref, hi_ref, lo_ref, yi_ref, yj_ref):
    a = dotf(lj_ref[col], hi_ref[...], NT)
    b = dotf(lj_ref[col, 0:64, :], lo_ref[...], NT)
    yi_ref[row] += md * (a[:64] + a[64:] + b)
    a = dotf(li_ref[row, :, 0:BLOCK], hi_ref[:, 0:BLOCK], NN) + dotf(li_ref[row, :, BLOCK:], hi_ref[:, BLOCK:], NN)
    b = dotf(li_ref[row, 0:64, 0:BLOCK], lo_ref[:, 0:BLOCK], NN) + dotf(
        li_ref[row, 0:64, BLOCK:], lo_ref[:, BLOCK:], NN)
    yj_ref[col] += mm * (a[:64] + a[64:] + b)


def compute_kernel(li, lj, p, q, table, other, yi_ref, yj_ref, counts, theirs, work, hi0, lo0, hi1, lo1, sem):
    _, z, core = place()
    loads = [pltpu.make_async_copy(table, counts, sem.at[0]), pltpu.make_async_copy(other, theirs, sem.at[1])]
    for cp in loads:
        cp.start()
    yi_ref[...] = jnp.zeros_like(yi_ref)
    yj_ref[...] = jnp.zeros_like(yj_ref)
    for cp in loads:
        cp.wait()

    gap = counts[15, 0] - theirs[15, 0]
    give = jnp.where(gap > 0, lax.shift_right_logical(gap, 1), 0)
    take = jnp.where(gap < 0, lax.shift_right_logical(-gap, 1), 0)

    def scan_own(ref, first, label, keep):
        def inner(n, passed):
            for i in range(2):
                for j in range(12):
                    m = ref[j, first + i]
                    work[n] = (label + i) * 4096 + j * 256 + m
                    live = m > 0
                    n = n + jnp.where(jnp.logical_and(live, keep(passed)), 1, 0)
                    passed = passed + jnp.where(live, 1, 0)
            return n
        return inner

    n = scan_own(counts, 2 * z, 2 * z, lambda k: k >= give)(jnp.int32(0), jnp.int32(0))
    n = scan_own(theirs, 2 * z, 2 * RING_LEN, lambda k: k < take)(n, jnp.int32(0))

    def scan_row(k, n):
        row = (2 * z + k) % (2 * RING_LEN)
        for j in range(12):
            m = counts[j, row]
            work[n] = row * 4096 + j * 256 + m
            n = n + jnp.where(m > 0, 1, 0)
        return n

    n = lax.fori_loop(2, 2 * RING_LEN, scan_row, n)
    for e in range(3):
        work[n + e] = 0

    def unpack(t):
        w = work[t]
        row = lax.shift_right_logical(w, 12)
        col = lax.shift_right_logical(w, 8) & 15
        m = w & 255
        owner = jnp.where(lax.shift_right_logical(row, 1) == RING_LEN, 1 - core, core)
        local = jnp.logical_or(lax.shift_right_logical(row, 1) == z, row >= 2 * RING_LEN)
        same = jnp.logical_and(local, col == owner * 2 + (row & 1))
        return row, col, m.astype(jnp.float32), jnp.where(same, 0, m).astype(jnp.float32)

    row, col, _, _ = unpack(0)
    build_tile(row, col, p, q, hi0, lo0)

    @pl.loop(0, (n + 1) // 2)
    def _(k):
        r0, c0, d0, m0 = unpack(2 * k)
        r1, c1, d1, m1 = unpack(2 * k + 1)
        r2, c2, _, _ = unpack(2 * k + 2)
        build_tile(r1, c1, p, q, hi1, lo1)
        apply_tile(r0, c0, d0, m0, li, lj, hi0, lo0, yi_ref, yj_ref)
        build_tile(r2, c2, p, q, hi0, lo0)
        apply_tile(r1, c1, d1, m1, li, lj, hi1, lo1, yi_ref, yj_ref)

    for i in range(2):
        yj_ref[2 * (1 - core) + i] += yi_ref[2 * RING_LEN + i]


def compute(li, lj, p, q, table, other):
    f = jnp.float32
    b = jnp.bfloat16
    return pl.pallas_call(
        compute_kernel,
        out_shape=(jax.ShapeDtypeStruct((18, 64, 256), f), jax.ShapeDtypeStruct((12, 64, 256), f)),
        in_specs=[VM] * 6, out_specs=(VM, VM),
        scratch_shapes=[pltpu.SMEM((16, 128), jnp.int32), pltpu.SMEM((16, 128), jnp.int32),
                        pltpu.SMEM((256,), jnp.int32),
                        pltpu.VMEM((256, 512), b), pltpu.VMEM((256, 512), b),
                        pltpu.VMEM((256, 512), b), pltpu.VMEM((256, 512), b),
                        pltpu.SemaphoreType.DMA((2,))],
        compiler_params=pltpu.CompilerParams(vmem_limit_bytes=24 << 20),
    )(li, lj, p, q, table, other)


PARTS = 4
SPAN = 64 // PARTS


def near(way, ch):
    return ch // (PARTS // 2) == way


def reduce_kernel(yi_ref, yj_ref, w_ref, out_ref, flow, side, ring_send, ring_recv, side_send, side_recv):
    ring, z, core = place()
    barrier = pltpu.get_barrier_semaphore()
    peers = partners(ring, z, core)
    for peer in peers:
        pl.semaphore_signal(barrier, inc=1, device_id=peer, device_id_type=MESH)
    pl.semaphore_wait(barrier, len(peers))
    started = []

    def part(ref, first, ch):
        return ref.at[pl.ds(first, 2), pl.ds(SPAN * ch, SPAN)]

    def hop(way, h, ch, src):
        return remote(src, part(flow.at[way, h], 0, ch), ring_send.at[way, h, ch], ring_recv.at[way, h, ch],
                      device(ring, z + 1 - 2 * way, core))

    def target(way, h):
        return (z + (1 - 2 * way) * (HOPS - h)) % RING_LEN

    def launch(cp):
        cp.start()
        started.append(cp)

    for ch in range(PARTS):
        for way in range(2):
            if near(way, ch):
                launch(hop(way, 0, ch, part(yi_ref, 2 * target(way, 0), ch)))
    for ch in range(PARTS):
        for way in range(2):
            if not near(way, ch):
                launch(hop(way, 1, ch, part(yi_ref, 2 * target(way, 1), ch)))
    n = 0
    for d in (1, 2):
        for c in range(2):
            launch(remote(yj_ref.at[pl.ds((d * 2 + c) * 2, 2)], side.at[(d - 1) * 2 + core], side_send.at[n],
                          side_recv.at[(d - 1) * 2 + core], device(ring + d, z, c)))
            n += 1
    launch(remote(yj_ref.at[pl.ds((1 - core) * 2, 2)], side.at[4], side_send.at[4], side_recv.at[4],
                  device(ring, z, 1 - core)))
    for h in range(1, HOPS):
        for first in (False, True):
            for ch in range(PARTS):
                for way in range(2):
                    if near(way, ch) != first or (h == 1 and not first):
                        continue
                    here = part(flow.at[way, h - 1], 0, ch)
                    hop(way, h - 1, ch, here).wait_recv()
                    rows = slice(SPAN * ch, SPAN * ch + SPAN)
                    flow[way, h - 1, :, rows, :] += yi_ref[pl.ds(2 * target(way, h), 2), rows, :]
                    launch(hop(way, h, ch, here))
    for way in range(2):
        for ch in range(PARTS):
            hop(way, HOPS - 1, ch, part(flow.at[way, 0], 0, ch)).wait_recv()
    for s in range(5):
        remote(side.at[s], side.at[s], side_send.at[s], side_recv.at[s], device(ring, z, 1 - core)).wait_recv()
    for h in range(2):
        total = yi_ref[2 * z + h] + yj_ref[2 * core + h]
        total += side[0, h] + side[1, h] + (side[2, h] + side[3, h]) + side[4, h]
        total += flow[0, HOPS - 1, h] + flow[1, HOPS - 1, h]
        out_ref[:, h * BLOCK:(h + 1) * BLOCK] = total * w_ref[0:1, h * BLOCK:(h + 1) * BLOCK]
    for cp in started:
        cp.wait_send()


def reduce(yi, yj, w):
    f = jnp.float32
    dma = pltpu.SemaphoreType.DMA
    return pl.pallas_call(
        reduce_kernel,
        out_shape=jax.ShapeDtypeStruct((64, 512), f),
        in_specs=[VM] * 3, out_specs=VM,
        scratch_shapes=[pltpu.VMEM((2, HOPS, 2, 64, 256), f), pltpu.VMEM((5, 2, 64, 256), f),
                        dma((2, HOPS, PARTS)), dma((2, HOPS, PARTS)), dma((5,)), dma((5,))],
        compiler_params=pltpu.CompilerParams(collective_id=1, has_side_effects=True, vmem_limit_bytes=16 << 20),
    )(yi, yj, w)


def body(drive, coords, rule_index, rule_weight, pair_cols, pair_count):
    held = [pltpu.with_memory_space_constraint(v, pltpu.HBM) for v in (
        drive.reshape(64, 512), coords, rule_index.reshape(1, 512), rule_weight, pair_cols.reshape(1, SLOTS))]
    li, lj, p, q, table, other, w = gather(*held, pair_count)
    yi, yj = compute(li, lj, p, q, table, other)
    return reduce(yi, yj, w).reshape(2, 32, 512)


def solution(mesh):
    both = ("band", "dev")
    in_specs = (P(None, None, both), P(None, both), P(both), P(), P(both), P(both))
    return jax.shard_map(body, mesh=mesh, in_specs=in_specs, out_specs=P(None, None, both), check_vma=False)
```

```python
import math

import jax
import jax.numpy as jnp
from jax import lax
from jax.experimental import pallas as pl
from jax.experimental.pallas import tpu as pltpu
from jax.sharding import PartitionSpec as P

BLOCK = 256
RULES = 4
SLOTS = 96
RINGS = 16
RING_LEN = 8
HOPS = 4
ROWS = 32
PACK = 72
WAVES = 25.0 / (2.0 * math.pi)
GAIN = 25.0 / (8.0 * math.pi**2)
SMOOTH = (0.05 * WAVES) ** 2
SINE = (2.6417539924711972, -1.0863767471480779, 0.1340056362838771, -0.007739908243745813)
FULL = 2.0 * math.sqrt(2.0)
HALF = math.sqrt(2.0)

VM = pl.BlockSpec(memory_space=pltpu.VMEM)
HBM = pl.BlockSpec(memory_space=pltpu.HBM)
MESH = pl.DeviceIdType.MESH
NT = (((1,), (1,)), ((), ()))
NN = (((1,), (0,)), ((), ()))


def place():
    me = lax.axis_index("band") * 32 + lax.axis_index("dev")
    return me // 16, (me // 2) % 8, me % 2


def device(ring, z, core):
    k = (ring % RINGS) * 16 + (z % RING_LEN) * 2 + core
    return (k // 32, k % 32)


def remote(src, dst, ssem, rsem, target):
    return pltpu.make_async_remote_copy(
        src_ref=src, dst_ref=dst, send_sem=ssem, recv_sem=rsem, device_id=target, device_id_type=MESH
    )


def partners(ring, z, core):
    peers = [device(ring, z + 1, core), device(ring, z - 1, core), device(ring, z, 1 - core)]
    for d in (1, -1, 2, -2):
        for c in range(2):
            peers.append(device(ring + d, z, c))
    return peers


def split(v):
    hi = v.astype(jnp.bfloat16)
    return hi, (v - hi.astype(jnp.float32)).astype(jnp.bfloat16)


def fill_vectors(src, slot, l_ref):
    for h in range(2):
        hi, lo = split(src[0:64, h * BLOCK:(h + 1) * BLOCK])
        k = 2 * slot + h
        l_ref[k, 0:64, 0:BLOCK] = hi
        l_ref[k, 64:128, 0:BLOCK] = lo
        l_ref[k, 0:32, BLOCK:] = -hi[32:]
        l_ref[k, 32:64, BLOCK:] = hi[:32]
        l_ref[k, 64:96, BLOCK:] = -lo[32:]
        l_ref[k, 96:128, BLOCK:] = lo[:32]


def far(way, ch):
    return ch // (NCH // 2) == way


CUTS = (0, 40, 72)
NCH = len(CUTS) - 1


def gather_kernel(x_hbm, c_hbm, rule_hbm, rw_hbm, cols_hbm, count_ref,
                  li_ref, lj_ref, p_ref, q_ref, table_ref, other_ref, w_ref,
                  b_ref, bi_ref, bj_ref, x_ref, c_ref, rule_ref, cols_ref, rw_ref,
                  seen_ref, ring_send, ring_recv, side_send, side_recv, load_sem, seen_sem):
    ring, z, core = place()
    loads = [pltpu.make_async_copy(src, dst, load_sem.at[n]) for n, (src, dst) in enumerate((
        (rule_hbm, rule_ref), (rw_hbm, rw_ref), (x_hbm, x_ref), (c_hbm, c_ref), (cols_hbm, cols_ref)))]
    for cp in loads:
        cp.start()
    barrier = pltpu.get_barrier_semaphore()
    peers = partners(ring, z, core)
    for peer in peers:
        pl.semaphore_signal(barrier, inc=1, device_id=peer, device_id_type=MESH)

    for cp in loads:
        cp.wait()
    rule = rule_ref[...]
    w = jnp.zeros((1, 512), jnp.float32)
    for r in range(RULES):
        w = jnp.where(rule == r, rw_ref[r], w)
    w_ref[...] = jnp.broadcast_to(w, (8, 512))
    b_ref[0:64, :] = x_ref[...] * (w * GAIN)
    b_ref[64:67, :] = c_ref[...] * WAVES
    b_ref[67:72, :] = jnp.full((5, 512), -2.0, jnp.float32)
    slot = lax.broadcasted_iota(jnp.int32, (1, SLOTS), 1)
    b_ref[67:68, 0:SLOTS] = jnp.where(slot < count_ref[0], cols_ref[...], -2).astype(jnp.float32)
    table_ref[...] = jnp.zeros_like(table_ref)

    pl.semaphore_wait(barrier, len(peers))
    started = []

    def launch(cp):
        cp.start()
        started.append(cp)

    def owner_of(way, h):
        return (z - (1 - 2 * way) * h) % RING_LEN

    def hop(way, h, ch):
        owner = owner_of(way, h)
        rows = pl.ds(CUTS[ch], CUTS[ch + 1] - CUTS[ch])
        src = b_ref.at[rows] if h == 0 else bi_ref.at[owner, rows]
        return remote(src, bi_ref.at[owner, rows], ring_send.at[way, h, ch], ring_recv.at[way, h, ch],
                      device(ring, z + 1 - 2 * way, core))

    for ch in range(NCH):
        for way in range(2):
            launch(hop(way, 0, ch))
    for n, (d, c) in enumerate(((1, 0), (1, 1), (2, 0), (2, 1))):
        launch(remote(b_ref, bj_ref.at[d * 2 + core], side_send.at[n],
                      side_recv.at[d * 2 + core], device(ring - d, z, c)))
    launch(remote(b_ref, bj_ref.at[core], side_send.at[4], side_recv.at[core],
                  device(ring, z, 1 - core)))

    lane = lax.broadcasted_iota(jnp.int32, (16, 128), 1)
    col = lax.broadcasted_iota(jnp.int32, (16, 128), 0)
    want = jnp.where(col < 12, (ring + col // 4) * 32 + z * 4 + col % 4, -1).astype(jnp.float32)

    def expand_i(src, k, listed=True):
        fill_vectors(src, k, li_ref)
        t = src[64:72, :].T
        for h in range(2):
            for d in range(3):
                p_ref[2 * k + h, d] = jnp.broadcast_to(t[h * BLOCK:(h + 1) * BLOCK, d:d + 1], (BLOCK, 128))
        if not listed:
            return
        hit = jnp.where(jnp.broadcast_to(src[67:68, 0:128], (16, 128)) == want, 1.0, 0.0)
        for i in range(2):
            m = jnp.sum(jnp.where(lane % 2 == i, hit, 0.0), axis=1, keepdims=True)
            table_ref[...] += jnp.where(lane == 2 * k + i, m, 0.0).astype(jnp.int32)

    def expand_j(src, k):
        fill_vectors(src, k, lj_ref)
        for h in range(2):
            q_ref[2 * k + h] = src[64:72, h * BLOCK:(h + 1) * BLOCK]

    expand_i(b_ref, z)
    expand_j(b_ref, core)
    for h in range(1, HOPS):
        for ch in range(NCH):
            for way in range(2):
                hop(way, h - 1, ch).wait_recv()
                if h < HOPS - 1 or far(way, ch):
                    launch(hop(way, h, ch))
        for way in range(2):
            k = owner_of(way, h)
            expand_i(bi_ref.at[k], k)
        js = ((1 - core, 4),) if h == 1 else ((4, 0), (5, 0)) if h == 2 else ((2, 0), (3, 0))
        for k, n in js:
            remote(b_ref, bj_ref.at[k], side_send.at[n], side_recv.at[k],
                   device(ring, z, 1 - core)).wait_recv()
            expand_j(bj_ref.at[k], k)
            if n == 4:
                expand_i(bj_ref.at[k], RING_LEN, listed=False)
        if h == HOPS - 1:
            have = table_ref[...]
            tally = jnp.sum(jnp.where(have > 0, 1.0, 0.0)).astype(jnp.int32)
            have = jnp.where(col == 15, tally, have)
            seen_ref[...] = have
            table_ref[...] = have
    note = remote(seen_ref, other_ref, seen_sem.at[0], seen_sem.at[1], device(ring, z, 1 - core))
    note.start()
    for way in range(2):
        for ch in range(NCH):
            if far(way, ch):
                hop(way, HOPS - 1, ch).wait_recv()
    k = (z + HOPS) % RING_LEN
    expand_i(bi_ref.at[k], k)
    note.wait()
    for cp in started:
        cp.wait_send()


def gather(x, coords, rule, rw, cols, count):
    f = jnp.float32
    b = jnp.bfloat16
    dma = pltpu.SemaphoreType.DMA
    s = jax.ShapeDtypeStruct
    return pl.pallas_call(
        gather_kernel,
        out_shape=(s((18, 128, 512), b), s((12, 128, 512), b), s((18, 3, 256, 128), f), s((12, 8, 256), f),
                   s((16, 128), jnp.int32), s((16, 128), jnp.int32), s((8, 512), f)),
        in_specs=[HBM] * 5 + [pl.BlockSpec(memory_space=pltpu.SMEM)],
        out_specs=(VM,) * 7,
        scratch_shapes=[pltpu.VMEM((PACK, 512), f), pltpu.VMEM((8, PACK, 512), f), pltpu.VMEM((6, PACK, 512), f),
                        pltpu.VMEM((64, 512), f), pltpu.VMEM((3, 512), f), pltpu.VMEM((1, 512), jnp.int32),
                        pltpu.VMEM((1, SLOTS), jnp.int32), pltpu.SMEM((RULES,), f), pltpu.VMEM((16, 128), jnp.int32),
                        dma((2, HOPS, NCH)), dma((2, HOPS, NCH)), dma((5,)), dma((6,)), dma((5,)), dma((2,))],
        compiler_params=pltpu.CompilerParams(collective_id=0, has_side_effects=True, vmem_limit_bytes=20 << 20),
    )(x, coords, rule, rw, cols, count)


def build_tile(row, col, p_ref, q_ref, hi_ref, lo_ref):
    qx = q_ref[col, 0:1, :]
    qy = q_ref[col, 1:2, :]
    qz = q_ref[col, 2:3, :]
    for r in range(0, BLOCK, ROWS):
        px = p_ref[row, 0, r:r + ROWS, :]
        py = p_ref[row, 1, r:r + ROWS, :]
        pz = p_ref[row, 2, r:r + ROWS, :]
        dx = jnp.concatenate([px, px], axis=1) - qx
        dy = jnp.concatenate([py, py], axis=1) - qy
        dz = jnp.concatenate([pz, pz], axis=1) - qz
        square = dx * dx + (dy * dy + (dz * dz + SMOOTH))
        inv = lax.rsqrt(square)
        turns = square * inv
        f = turns - jnp.round(turns)
        f2 = f * f
        poly = SINE[-1]
        for k in SINE[-2::-1]:
            poly = poly * f2 + k
        s = f * poly
        ss = s * s
        rest = FULL - ss
        sh = s * (rest * lax.rsqrt(rest))
        ch = HALF - ss
        t = inv * sh
        rh, rl = split(inv - t * sh)
        ih, il = split(t * ch)
        hi_ref[r:r + ROWS, 0:BLOCK] = rh
        hi_ref[r:r + ROWS, BLOCK:] = ih
        lo_ref[r:r + ROWS, 0:BLOCK] = rl
        lo_ref[r:r + ROWS, BLOCK:] = il


def dotf(a, b, dims):
    return lax.dot_general(a, b, dims, preferred_element_type=jnp.float32)


def apply_tile(row, col, md, mm, li_ref, lj_ref, hi_ref, lo_ref, yi_ref, yj_ref):
    a = dotf(lj_ref[col], hi_ref[...], NT)
    b = dotf(lj_ref[col, 0:64, :], lo_ref[...], NT)
    yi_ref[row] += md * (a[:64] + a[64:] + b)
    a = dotf(li_ref[row, :, 0:BLOCK], hi_ref[:, 0:BLOCK], NN) + dotf(li_ref[row, :, BLOCK:], hi_ref[:, BLOCK:], NN)
    b = dotf(li_ref[row, 0:64, 0:BLOCK], lo_ref[:, 0:BLOCK], NN) + dotf(
        li_ref[row, 0:64, BLOCK:], lo_ref[:, BLOCK:], NN)
    yj_ref[col] += mm * (a[:64] + a[64:] + b)


def compute_kernel(li, lj, p, q, table, other, yi_ref, yj_ref, counts, theirs, work, hi0, lo0, hi1, lo1, sem):
    _, z, core = place()
    loads = [pltpu.make_async_copy(table, counts, sem.at[0]), pltpu.make_async_copy(other, theirs, sem.at[1])]
    for cp in loads:
        cp.start()
    yi_ref[...] = jnp.zeros_like(yi_ref)
    yj_ref[...] = jnp.zeros_like(yj_ref)
    build_tile(2 * z, 2 * core, p, q, hi0, lo0)
    for cp in loads:
        cp.wait()

    gap = counts[15, 0] - theirs[15, 0]
    give = jnp.where(gap > 0, lax.shift_right_logical(gap, 1), 0)
    take = jnp.where(gap < 0, lax.shift_right_logical(-gap, 1), 0)

    def scan_own(ref, first, label, keep):
        def inner(n, passed):
            for i in range(2):
                for j in range(12):
                    m = ref[j, first + i]
                    work[n] = (label + i) * 4096 + j * 256 + m
                    live = m > 0
                    n = n + jnp.where(jnp.logical_and(live, keep(passed)), 1, 0)
                    passed = passed + jnp.where(live, 1, 0)
            return n
        return inner

    n = scan_own(counts, 2 * z, 2 * z, lambda k: jnp.logical_or(k == 0, k > give))(jnp.int32(0), jnp.int32(0))
    n = scan_own(theirs, 2 * z, 2 * RING_LEN, lambda k: jnp.logical_and(k > 0, k <= take))(n, jnp.int32(0))

    def scan_row(k, n):
        row = (2 * z + k) % (2 * RING_LEN)
        base = jnp.where(row > 2 * z, 4, 0)
        for j in range(8):
            m = counts[base + j, row]
            work[n] = row * 4096 + (base + j) * 256 + m
            n = n + jnp.where(m > 0, 1, 0)
        return n

    n = lax.fori_loop(2, 2 * RING_LEN, scan_row, n)
    for e in range(3):
        work[n + e] = 0

    def unpack(t):
        w = work[t]
        row = lax.shift_right_logical(w, 12)
        col = lax.shift_right_logical(w, 8) & 15
        m = w & 255
        owner = jnp.where(lax.shift_right_logical(row, 1) == RING_LEN, 1 - core, core)
        local = jnp.logical_or(lax.shift_right_logical(row, 1) == z, row >= 2 * RING_LEN)
        same = jnp.logical_and(local, col == owner * 2 + (row & 1))
        return row, col, m.astype(jnp.float32), jnp.where(same, 0, m).astype(jnp.float32)


    @pl.loop(0, (n + 1) // 2)
    def _(k):
        r0, c0, d0, m0 = unpack(2 * k)
        r1, c1, d1, m1 = unpack(2 * k + 1)
        r2, c2, _, _ = unpack(2 * k + 2)
        build_tile(r1, c1, p, q, hi1, lo1)
        apply_tile(r0, c0, d0, m0, li, lj, hi0, lo0, yi_ref, yj_ref)
        build_tile(r2, c2, p, q, hi0, lo0)
        apply_tile(r1, c1, d1, m1, li, lj, hi1, lo1, yi_ref, yj_ref)

    for i in range(2):
        yj_ref[2 * (1 - core) + i] += yi_ref[2 * RING_LEN + i]


def compute(li, lj, p, q, table, other):
    f = jnp.float32
    b = jnp.bfloat16
    return pl.pallas_call(
        compute_kernel,
        out_shape=(jax.ShapeDtypeStruct((18, 64, 256), f), jax.ShapeDtypeStruct((12, 64, 256), f)),
        in_specs=[VM] * 6, out_specs=(VM, VM),
        scratch_shapes=[pltpu.SMEM((16, 128), jnp.int32), pltpu.SMEM((16, 128), jnp.int32),
                        pltpu.SMEM((256,), jnp.int32),
                        pltpu.VMEM((256, 512), b), pltpu.VMEM((256, 512), b),
                        pltpu.VMEM((256, 512), b), pltpu.VMEM((256, 512), b),
                        pltpu.SemaphoreType.DMA((2,))],
        compiler_params=pltpu.CompilerParams(vmem_limit_bytes=24 << 20),
    )(li, lj, p, q, table, other)


PARTS = 4
SPAN = 64 // PARTS


def near(way, ch):
    return ch // (PARTS // 2) == way


def reduce_kernel(yi_ref, yj_ref, w_ref, out_ref, flow, side, ring_send, ring_recv, side_send, side_recv):
    ring, z, core = place()
    barrier = pltpu.get_barrier_semaphore()
    peers = partners(ring, z, core)
    for peer in peers:
        pl.semaphore_signal(barrier, inc=1, device_id=peer, device_id_type=MESH)
    pl.semaphore_wait(barrier, len(peers))
    started = []

    def part(ref, first, ch):
        return ref.at[pl.ds(first, 2), pl.ds(SPAN * ch, SPAN)]

    def hop(way, h, ch, src):
        return remote(src, part(flow.at[way, h], 0, ch), ring_send.at[way, h, ch], ring_recv.at[way, h, ch],
                      device(ring, z + 1 - 2 * way, core))

    def target(way, h):
        return (z + (1 - 2 * way) * (HOPS - h)) % RING_LEN

    def launch(cp):
        cp.start()
        started.append(cp)

    for ch in range(PARTS):
        for way in range(2):
            if near(way, ch):
                launch(hop(way, 0, ch, part(yi_ref, 2 * target(way, 0), ch)))
    for ch in range(PARTS):
        for way in range(2):
            if not near(way, ch):
                launch(hop(way, 1, ch, part(yi_ref, 2 * target(way, 1), ch)))
    n = 0
    for d in (1, 2):
        for c in range(2):
            launch(remote(yj_ref.at[pl.ds((d * 2 + c) * 2, 2)], side.at[(d - 1) * 2 + core], side_send.at[n],
                          side_recv.at[(d - 1) * 2 + core], device(ring + d, z, c)))
            n += 1
    launch(remote(yj_ref.at[pl.ds((1 - core) * 2, 2)], side.at[4], side_send.at[4], side_recv.at[4],
                  device(ring, z, 1 - core)))
    for h in range(1, HOPS):
        for first in (False, True):
            for ch in range(PARTS):
                for way in range(2):
                    if near(way, ch) != first or (h == 1 and not first):
                        continue
                    here = part(flow.at[way, h - 1], 0, ch)
                    hop(way, h - 1, ch, here).wait_recv()
                    rows = slice(SPAN * ch, SPAN * ch + SPAN)
                    flow[way, h - 1, :, rows, :] += yi_ref[pl.ds(2 * target(way, h), 2), rows, :]
                    launch(hop(way, h, ch, here))
    for way in range(2):
        for ch in range(PARTS):
            hop(way, HOPS - 1, ch, part(flow.at[way, 0], 0, ch)).wait_recv()
    for s in range(5):
        remote(side.at[s], side.at[s], side_send.at[s], side_recv.at[s], device(ring, z, 1 - core)).wait_recv()
    for h in range(2):
        total = yi_ref[2 * z + h] + yj_ref[2 * core + h]
        total += side[0, h] + side[1, h] + (side[2, h] + side[3, h]) + side[4, h]
        total += flow[0, HOPS - 1, h] + flow[1, HOPS - 1, h]
        out_ref[:, h * BLOCK:(h + 1) * BLOCK] = total * w_ref[0:1, h * BLOCK:(h + 1) * BLOCK]
    for cp in started:
        cp.wait_send()


def reduce(yi, yj, w):
    f = jnp.float32
    dma = pltpu.SemaphoreType.DMA
    return pl.pallas_call(
        reduce_kernel,
        out_shape=jax.ShapeDtypeStruct((64, 512), f),
        in_specs=[VM] * 3, out_specs=VM,
        scratch_shapes=[pltpu.VMEM((2, HOPS, 2, 64, 256), f), pltpu.VMEM((5, 2, 64, 256), f),
                        dma((2, HOPS, PARTS)), dma((2, HOPS, PARTS)), dma((5,)), dma((5,))],
        compiler_params=pltpu.CompilerParams(collective_id=1, has_side_effects=True, vmem_limit_bytes=16 << 20),
    )(yi, yj, w)


def body(drive, coords, rule_index, rule_weight, pair_cols, pair_count):
    held = [pltpu.with_memory_space_constraint(v, pltpu.HBM) for v in (
        drive.reshape(64, 512), coords, rule_index.reshape(1, 512), rule_weight, pair_cols.reshape(1, SLOTS))]
    li, lj, p, q, table, other, w = gather(*held, pair_count)
    yi, yj = compute(li, lj, p, q, table, other)
    return reduce(yi, yj, w).reshape(2, 32, 512)


def solution(mesh):
    both = ("band", "dev")
    in_specs = (P(None, None, both), P(None, both), P(both), P(), P(both), P(both))
    return jax.shard_map(body, mesh=mesh, in_specs=in_specs, out_specs=P(None, None, both), check_vma=False)
```

```python
import math

import jax
import jax.numpy as jnp
from jax import lax
from jax.experimental import pallas as pl
from jax.experimental.pallas import tpu as pltpu
from jax.sharding import PartitionSpec as P

BLOCK = 256
RULES = 4
SLOTS = 96
RINGS = 16
RING_LEN = 8
HOPS = 4
ROWS = 32
PACK = 72
WAVES = 25.0 / (2.0 * math.pi)
GAIN = 25.0 / (8.0 * math.pi**2)
SMOOTH = (0.05 * WAVES) ** 2
SINE = (2.6417539924711972, -1.0863767471480779, 0.1340056362838771, -0.007739908243745813)
FULL = 2.0 * math.sqrt(2.0)
HALF = math.sqrt(2.0)

VM = pl.BlockSpec(memory_space=pltpu.VMEM)
HBM = pl.BlockSpec(memory_space=pltpu.HBM)
MESH = pl.DeviceIdType.MESH
NT = (((1,), (1,)), ((), ()))
NN = (((1,), (0,)), ((), ()))


def place():
    me = lax.axis_index("band") * 32 + lax.axis_index("dev")
    return me // 16, (me // 2) % 8, me % 2


def device(ring, z, core):
    k = (ring % RINGS) * 16 + (z % RING_LEN) * 2 + core
    return (k // 32, k % 32)


def remote(src, dst, ssem, rsem, target):
    return pltpu.make_async_remote_copy(
        src_ref=src, dst_ref=dst, send_sem=ssem, recv_sem=rsem, device_id=target, device_id_type=MESH
    )


def partners(ring, z, core):
    peers = [device(ring, z + 1, core), device(ring, z - 1, core), device(ring, z, 1 - core)]
    for d in (1, -1, 2, -2):
        for c in range(2):
            peers.append(device(ring + d, z, c))
    return peers


def split(v):
    hi = v.astype(jnp.bfloat16)
    return hi, (v - hi.astype(jnp.float32)).astype(jnp.bfloat16)


def fill_vectors(src, slot, l_ref):
    for h in range(2):
        hi, lo = split(src[0:64, h * BLOCK:(h + 1) * BLOCK])
        k = 2 * slot + h
        l_ref[k, 0:64, 0:BLOCK] = hi
        l_ref[k, 64:128, 0:BLOCK] = lo
        l_ref[k, 0:32, BLOCK:] = -hi[32:]
        l_ref[k, 32:64, BLOCK:] = hi[:32]
        l_ref[k, 64:96, BLOCK:] = -lo[32:]
        l_ref[k, 96:128, BLOCK:] = lo[:32]


def far(way, ch):
    return ch // (NCH // 2) == way


CUTS = (0, 40, 72)
NCH = len(CUTS) - 1


def gather_kernel(x_hbm, c_hbm, rule_hbm, rw_hbm, cols_hbm, count_ref,
                  li_ref, lj_ref, p_ref, q_ref, table_ref, other_ref, w_ref,
                  b_ref, bi_ref, bj_ref, x_ref, c_ref, rule_ref, cols_ref, rw_ref,
                  seen_ref, ring_send, ring_recv, side_send, side_recv, load_sem, seen_sem):
    ring, z, core = place()
    loads = [pltpu.make_async_copy(src, dst, load_sem.at[n]) for n, (src, dst) in enumerate((
        (rule_hbm, rule_ref), (rw_hbm, rw_ref), (x_hbm, x_ref), (c_hbm, c_ref), (cols_hbm, cols_ref)))]
    for cp in loads:
        cp.start()
    barrier = pltpu.get_barrier_semaphore()
    peers = partners(ring, z, core)
    for peer in peers:
        pl.semaphore_signal(barrier, inc=1, device_id=peer, device_id_type=MESH)

    for cp in loads:
        cp.wait()
    rule = rule_ref[...]
    w = jnp.zeros((1, 512), jnp.float32)
    for r in range(RULES):
        w = jnp.where(rule == r, rw_ref[r], w)
    w_ref[...] = jnp.broadcast_to(w, (8, 512))
    b_ref[0:64, :] = x_ref[...] * (w * GAIN)
    b_ref[64:67, :] = c_ref[...] * WAVES
    b_ref[67:72, :] = jnp.full((5, 512), -2.0, jnp.float32)
    slot = lax.broadcasted_iota(jnp.int32, (1, SLOTS), 1)
    b_ref[67:68, 0:SLOTS] = jnp.where(slot < count_ref[0], cols_ref[...], -2).astype(jnp.float32)
    table_ref[...] = jnp.zeros_like(table_ref)

    pl.semaphore_wait(barrier, len(peers))
    started = []

    def launch(cp):
        cp.start()
        started.append(cp)

    def owner_of(way, h):
        return (z - (1 - 2 * way) * h) % RING_LEN

    def hop(way, h, ch):
        owner = owner_of(way, h)
        rows = pl.ds(CUTS[ch], CUTS[ch + 1] - CUTS[ch])
        src = b_ref.at[rows] if h == 0 else bi_ref.at[owner, rows]
        return remote(src, bi_ref.at[owner, rows], ring_send.at[way, h, ch], ring_recv.at[way, h, ch],
                      device(ring, z + 1 - 2 * way, core))

    for ch in range(NCH):
        for way in range(2):
            launch(hop(way, 0, ch))
    for n, (d, c) in enumerate(((1, 0), (1, 1), (2, 0), (2, 1))):
        launch(remote(b_ref, bj_ref.at[d * 2 + core], side_send.at[n],
                      side_recv.at[d * 2 + core], device(ring - d, z, c)))
    launch(remote(b_ref, bj_ref.at[core], side_send.at[4], side_recv.at[core],
                  device(ring, z, 1 - core)))

    lane = lax.broadcasted_iota(jnp.int32, (16, 128), 1)
    col = lax.broadcasted_iota(jnp.int32, (16, 128), 0)
    want = jnp.where(col < 12, (ring + col // 4) * 32 + z * 4 + col % 4, -1).astype(jnp.float32)

    def expand_i(src, k, listed=True):
        fill_vectors(src, k, li_ref)
        t = src[64:72, :].T
        for h in range(2):
            for d in range(3):
                p_ref[2 * k + h, d] = jnp.broadcast_to(t[h * BLOCK:(h + 1) * BLOCK, d:d + 1], (BLOCK, 128))
        if not listed:
            return
        hit = jnp.where(jnp.broadcast_to(src[67:68, 0:128], (16, 128)) == want, 1.0, 0.0)
        for i in range(2):
            m = jnp.sum(jnp.where(lane % 2 == i, hit, 0.0), axis=1, keepdims=True)
            table_ref[...] += jnp.where(lane == 2 * k + i, m, 0.0).astype(jnp.int32)

    def expand_j(src, k):
        fill_vectors(src, k, lj_ref)
        for h in range(2):
            q_ref[2 * k + h] = src[64:72, h * BLOCK:(h + 1) * BLOCK]

    expand_i(b_ref, z)
    expand_j(b_ref, core)
    for h in range(1, HOPS):
        for ch in range(NCH):
            for way in range(2):
                hop(way, h - 1, ch).wait_recv()
                if h < HOPS - 1 or far(way, ch):
                    launch(hop(way, h, ch))
        for way in range(2):
            k = owner_of(way, h)
            expand_i(bi_ref.at[k], k)
        js = ((1 - core, 4),) if h == 1 else ((4, 0), (5, 0)) if h == 2 else ((2, 0), (3, 0))
        for k, n in js:
            remote(b_ref, bj_ref.at[k], side_send.at[n], side_recv.at[k],
                   device(ring, z, 1 - core)).wait_recv()
            expand_j(bj_ref.at[k], k)
            if n == 4:
                expand_i(bj_ref.at[k], RING_LEN, listed=False)
        if h == HOPS - 1:
            have = table_ref[...]
            tally = jnp.sum(jnp.where(have > 0, 1.0, 0.0)).astype(jnp.int32)
            have = jnp.where(col == 15, tally, have)
            seen_ref[...] = have
            table_ref[...] = have
    note = remote(seen_ref, other_ref, seen_sem.at[0], seen_sem.at[1], device(ring, z, 1 - core))
    note.start()
    for way in range(2):
        for ch in range(NCH):
            if far(way, ch):
                hop(way, HOPS - 1, ch).wait_recv()
    k = (z + HOPS) % RING_LEN
    expand_i(bi_ref.at[k], k)
    note.wait()
    for cp in started:
        cp.wait_send()


def gather(x, coords, rule, rw, cols, count):
    f = jnp.float32
    b = jnp.bfloat16
    dma = pltpu.SemaphoreType.DMA
    s = jax.ShapeDtypeStruct
    return pl.pallas_call(
        gather_kernel,
        out_shape=(s((18, 128, 512), b), s((12, 128, 512), b), s((18, 3, 256, 128), f), s((12, 8, 256), f),
                   s((16, 128), jnp.int32), s((16, 128), jnp.int32), s((8, 512), f)),
        in_specs=[HBM] * 5 + [pl.BlockSpec(memory_space=pltpu.SMEM)],
        out_specs=(VM,) * 7,
        scratch_shapes=[pltpu.VMEM((PACK, 512), f), pltpu.VMEM((8, PACK, 512), f), pltpu.VMEM((6, PACK, 512), f),
                        pltpu.VMEM((64, 512), f), pltpu.VMEM((3, 512), f), pltpu.VMEM((1, 512), jnp.int32),
                        pltpu.VMEM((1, SLOTS), jnp.int32), pltpu.SMEM((RULES,), f), pltpu.VMEM((16, 128), jnp.int32),
                        dma((2, HOPS, NCH)), dma((2, HOPS, NCH)), dma((5,)), dma((6,)), dma((5,)), dma((2,))],
        compiler_params=pltpu.CompilerParams(collective_id=0, has_side_effects=True, vmem_limit_bytes=20 << 20),
    )(x, coords, rule, rw, cols, count)


def build_tile(row, col, p_ref, q_ref, hi_ref, lo_ref):
    qx = q_ref[col, 0:1, :]
    qy = q_ref[col, 1:2, :]
    qz = q_ref[col, 2:3, :]
    for r in range(0, BLOCK, ROWS):
        px = p_ref[row, 0, r:r + ROWS, :]
        py = p_ref[row, 1, r:r + ROWS, :]
        pz = p_ref[row, 2, r:r + ROWS, :]
        dx = jnp.concatenate([px, px], axis=1) - qx
        dy = jnp.concatenate([py, py], axis=1) - qy
        dz = jnp.concatenate([pz, pz], axis=1) - qz
        square = dx * dx + (dy * dy + (dz * dz + SMOOTH))
        inv = lax.rsqrt(square)
        turns = square * inv
        f = turns - jnp.round(turns)
        f2 = f * f
        poly = SINE[-1]
        for k in SINE[-2::-1]:
            poly = poly * f2 + k
        s = f * poly
        ss = s * s
        rest = FULL - ss
        sh = s * (rest * lax.rsqrt(rest))
        ch = HALF - ss
        t = inv * sh
        rh, rl = split(inv - t * sh)
        ih, il = split(t * ch)
        hi_ref[r:r + ROWS, 0:BLOCK] = rh
        hi_ref[r:r + ROWS, BLOCK:] = ih
        lo_ref[r:r + ROWS, 0:BLOCK] = rl
        lo_ref[r:r + ROWS, BLOCK:] = il


def dotf(a, b, dims):
    return lax.dot_general(a, b, dims, preferred_element_type=jnp.float32)


def apply_tile(row, col, md, mm, li_ref, lj_ref, hi_ref, lo_ref, yi_ref, yj_ref):
    a = dotf(lj_ref[col], hi_ref[...], NT)
    b = dotf(lj_ref[col, 0:64, :], lo_ref[...], NT)
    yi_ref[row] += md * (a[:64] + a[64:] + b)
    a = dotf(li_ref[row, :, 0:BLOCK], hi_ref[:, 0:BLOCK], NN) + dotf(li_ref[row, :, BLOCK:], hi_ref[:, BLOCK:], NN)
    b = dotf(li_ref[row, 0:64, 0:BLOCK], lo_ref[:, 0:BLOCK], NN) + dotf(
        li_ref[row, 0:64, BLOCK:], lo_ref[:, BLOCK:], NN)
    yj_ref[col] += mm * (a[:64] + a[64:] + b)


def compute_kernel(li, lj, p, q, table, other, yi_ref, yj_ref, counts, theirs, work, hi0, lo0, hi1, lo1, sem):
    _, z, core = place()
    loads = [pltpu.make_async_copy(table, counts, sem.at[0]), pltpu.make_async_copy(other, theirs, sem.at[1])]
    for cp in loads:
        cp.start()
    yi_ref[...] = jnp.zeros_like(yi_ref)
    yj_ref[...] = jnp.zeros_like(yj_ref)
    build_tile(2 * z, 2 * core, p, q, hi0, lo0)
    for cp in loads:
        cp.wait()

    gap = counts[15, 0] - theirs[15, 0]
    give = jnp.where(gap > 0, lax.shift_right_logical(gap, 1), 0)
    take = jnp.where(gap < 0, lax.shift_right_logical(-gap, 1), 0)

    def scan_own(ref, first, label, keep):
        def inner(n, passed):
            for i in range(2):
                for j in range(12):
                    m = ref[j, first + i]
                    work[n] = (label + i) * 4096 + j * 256 + m
                    live = m > 0
                    n = n + jnp.where(jnp.logical_and(live, keep(passed)), 1, 0)
                    passed = passed + jnp.where(live, 1, 0)
            return n
        return inner

    n = scan_own(counts, 2 * z, 2 * z, lambda k: jnp.logical_or(k == 0, k > give))(jnp.int32(0), jnp.int32(0))
    n = scan_own(theirs, 2 * z, 2 * RING_LEN, lambda k: jnp.logical_and(k > 0, k <= take))(n, jnp.int32(0))

    def scan_row(k, n):
        row = (2 * z + k) % (2 * RING_LEN)
        base = jnp.where(row > 2 * z, 4, 0)
        for j in range(8):
            m = counts[base + j, row]
            work[n] = row * 4096 + (base + j) * 256 + m
            n = n + jnp.where(m > 0, 1, 0)
        return n

    n = lax.fori_loop(2, 2 * RING_LEN, scan_row, n)
    for e in range(3):
        work[n + e] = 0

    def unpack(t):
        w = work[t]
        row = lax.shift_right_logical(w, 12)
        col = lax.shift_right_logical(w, 8) & 15
        m = w & 255
        owner = jnp.where(lax.shift_right_logical(row, 1) == RING_LEN, 1 - core, core)
        local = jnp.logical_or(lax.shift_right_logical(row, 1) == z, row >= 2 * RING_LEN)
        same = jnp.logical_and(local, col == owner * 2 + (row & 1))
        return row, col, m.astype(jnp.float32), jnp.where(same, 0, m).astype(jnp.float32)


    @pl.loop(0, n // 2)
    def _(k):
        r0, c0, d0, m0 = unpack(2 * k)
        r1, c1, d1, m1 = unpack(2 * k + 1)
        r2, c2, _, _ = unpack(2 * k + 2)
        build_tile(r1, c1, p, q, hi1, lo1)
        apply_tile(r0, c0, d0, m0, li, lj, hi0, lo0, yi_ref, yj_ref)
        build_tile(r2, c2, p, q, hi0, lo0)
        apply_tile(r1, c1, d1, m1, li, lj, hi1, lo1, yi_ref, yj_ref)

    @pl.when(n % 2 == 1)
    def _():
        row, col, md, mm = unpack(n - 1)
        apply_tile(row, col, md, mm, li, lj, hi0, lo0, yi_ref, yj_ref)

    for i in range(2):
        yj_ref[2 * (1 - core) + i] += yi_ref[2 * RING_LEN + i]


def compute(li, lj, p, q, table, other):
    f = jnp.float32
    b = jnp.bfloat16
    return pl.pallas_call(
        compute_kernel,
        out_shape=(jax.ShapeDtypeStruct((18, 64, 256), f), jax.ShapeDtypeStruct((12, 64, 256), f)),
        in_specs=[VM] * 6, out_specs=(VM, VM),
        scratch_shapes=[pltpu.SMEM((16, 128), jnp.int32), pltpu.SMEM((16, 128), jnp.int32),
                        pltpu.SMEM((256,), jnp.int32),
                        pltpu.VMEM((256, 512), b), pltpu.VMEM((256, 512), b),
                        pltpu.VMEM((256, 512), b), pltpu.VMEM((256, 512), b),
                        pltpu.SemaphoreType.DMA((2,))],
        compiler_params=pltpu.CompilerParams(vmem_limit_bytes=24 << 20),
    )(li, lj, p, q, table, other)


PARTS = 4
SPAN = 64 // PARTS


def near(way, ch):
    return ch // (PARTS // 2) == way


def reduce_kernel(yi_ref, yj_ref, w_ref, out_ref, flow, side, ring_send, ring_recv, side_send, side_recv):
    ring, z, core = place()
    barrier = pltpu.get_barrier_semaphore()
    peers = partners(ring, z, core)
    for peer in peers:
        pl.semaphore_signal(barrier, inc=1, device_id=peer, device_id_type=MESH)
    pl.semaphore_wait(barrier, len(peers))
    started = []

    def part(ref, first, ch):
        return ref.at[pl.ds(first, 2), pl.ds(SPAN * ch, SPAN)]

    def hop(way, h, ch, src):
        return remote(src, part(flow.at[way, h], 0, ch), ring_send.at[way, h, ch], ring_recv.at[way, h, ch],
                      device(ring, z + 1 - 2 * way, core))

    def target(way, h):
        return (z + (1 - 2 * way) * (HOPS - h)) % RING_LEN

    def launch(cp):
        cp.start()
        started.append(cp)

    for ch in range(PARTS):
        for way in range(2):
            if near(way, ch):
                launch(hop(way, 0, ch, part(yi_ref, 2 * target(way, 0), ch)))
    for ch in range(PARTS):
        for way in range(2):
            if not near(way, ch):
                launch(hop(way, 1, ch, part(yi_ref, 2 * target(way, 1), ch)))
    n = 0
    for d in (1, 2):
        for c in range(2):
            launch(remote(yj_ref.at[pl.ds((d * 2 + c) * 2, 2)], side.at[(d - 1) * 2 + core], side_send.at[n],
                          side_recv.at[(d - 1) * 2 + core], device(ring + d, z, c)))
            n += 1
    launch(remote(yj_ref.at[pl.ds((1 - core) * 2, 2)], side.at[4], side_send.at[4], side_recv.at[4],
                  device(ring, z, 1 - core)))
    for h in range(1, HOPS):
        for first in (False, True):
            for ch in range(PARTS):
                for way in range(2):
                    if near(way, ch) != first or (h == 1 and not first):
                        continue
                    here = part(flow.at[way, h - 1], 0, ch)
                    hop(way, h - 1, ch, here).wait_recv()
                    rows = slice(SPAN * ch, SPAN * ch + SPAN)
                    flow[way, h - 1, :, rows, :] += yi_ref[pl.ds(2 * target(way, h), 2), rows, :]
                    launch(hop(way, h, ch, here))
    for way in range(2):
        for ch in range(PARTS):
            hop(way, HOPS - 1, ch, part(flow.at[way, 0], 0, ch)).wait_recv()
    for s in range(5):
        remote(side.at[s], side.at[s], side_send.at[s], side_recv.at[s], device(ring, z, 1 - core)).wait_recv()
    for h in range(2):
        total = yi_ref[2 * z + h] + yj_ref[2 * core + h]
        total += side[0, h] + side[1, h] + (side[2, h] + side[3, h]) + side[4, h]
        total += flow[0, HOPS - 1, h] + flow[1, HOPS - 1, h]
        out_ref[:, h * BLOCK:(h + 1) * BLOCK] = total * w_ref[0:1, h * BLOCK:(h + 1) * BLOCK]
    for cp in started:
        cp.wait_send()


def reduce(yi, yj, w):
    f = jnp.float32
    dma = pltpu.SemaphoreType.DMA
    return pl.pallas_call(
        reduce_kernel,
        out_shape=jax.ShapeDtypeStruct((64, 512), f),
        in_specs=[VM] * 3, out_specs=VM,
        scratch_shapes=[pltpu.VMEM((2, HOPS, 2, 64, 256), f), pltpu.VMEM((5, 2, 64, 256), f),
                        dma((2, HOPS, PARTS)), dma((2, HOPS, PARTS)), dma((5,)), dma((5,))],
        compiler_params=pltpu.CompilerParams(collective_id=1, has_side_effects=True, vmem_limit_bytes=16 << 20),
    )(yi, yj, w)


def body(drive, coords, rule_index, rule_weight, pair_cols, pair_count):
    held = [pltpu.with_memory_space_constraint(v, pltpu.HBM) for v in (
        drive.reshape(64, 512), coords, rule_index.reshape(1, 512), rule_weight, pair_cols.reshape(1, SLOTS))]
    li, lj, p, q, table, other, w = gather(*held, pair_count)
    yi, yj = compute(li, lj, p, q, table, other)
    return reduce(yi, yj, w).reshape(2, 32, 512)


def solution(mesh):
    both = ("band", "dev")
    in_specs = (P(None, None, both), P(None, both), P(both), P(), P(both), P(both))
    return jax.shard_map(body, mesh=mesh, in_specs=in_specs, out_specs=P(None, None, both), check_vma=False)
```

```python
import math

import jax
import jax.numpy as jnp
from jax import lax
from jax.experimental import pallas as pl
from jax.experimental.pallas import tpu as pltpu
from jax.sharding import PartitionSpec as P

BLOCK = 256
RULES = 4
SLOTS = 96
RINGS = 16
RING_LEN = 8
HOPS = 4
ROWS = 32
PACK = 72
WAVES = 25.0 / (2.0 * math.pi)
GAIN = 25.0 / (8.0 * math.pi**2)
SMOOTH = (0.05 * WAVES) ** 2
SINE = (2.6417539924711972, -1.0863767471480779, 0.1340056362838771, -0.007739908243745813)
FULL = 2.0 * math.sqrt(2.0)
HALF = math.sqrt(2.0)

VM = pl.BlockSpec(memory_space=pltpu.VMEM)
HBM = pl.BlockSpec(memory_space=pltpu.HBM)
MESH = pl.DeviceIdType.MESH
NT = (((1,), (1,)), ((), ()))
NN = (((1,), (0,)), ((), ()))


def place():
    me = lax.axis_index("band") * 32 + lax.axis_index("dev")
    return me // 16, (me // 2) % 8, me % 2


def device(ring, z, core):
    k = (ring % RINGS) * 16 + (z % RING_LEN) * 2 + core
    return (k // 32, k % 32)


def remote(src, dst, ssem, rsem, target):
    return pltpu.make_async_remote_copy(
        src_ref=src, dst_ref=dst, send_sem=ssem, recv_sem=rsem, device_id=target, device_id_type=MESH
    )


def partners(ring, z, core):
    peers = [device(ring, z + 1, core), device(ring, z - 1, core), device(ring, z, 1 - core)]
    for d in (1, -1, 2, -2):
        for c in range(2):
            peers.append(device(ring + d, z, c))
    return peers


def split(v):
    hi = v.astype(jnp.bfloat16)
    return hi, (v - hi.astype(jnp.float32)).astype(jnp.bfloat16)


def fill_vectors(src, slot, l_ref):
    for h in range(2):
        hi, lo = split(src[0:64, h * BLOCK:(h + 1) * BLOCK])
        k = 2 * slot + h
        l_ref[k, 0:64, 0:BLOCK] = hi
        l_ref[k, 64:128, 0:BLOCK] = lo
        l_ref[k, 0:32, BLOCK:] = -hi[32:]
        l_ref[k, 32:64, BLOCK:] = hi[:32]
        l_ref[k, 64:96, BLOCK:] = -lo[32:]
        l_ref[k, 96:128, BLOCK:] = lo[:32]


def far(way, ch):
    return ch // (NCH // 2) == way


CUTS = (0, 40, 72)
NCH = len(CUTS) - 1


def gather_kernel(x_hbm, c_hbm, rule_hbm, rw_hbm, cols_hbm, count_ref,
                  li_ref, lj_ref, p_ref, q_ref, table_ref, other_ref, w_ref,
                  b_ref, bi_ref, bj_ref, x_ref, c_ref, rule_ref, cols_ref, rw_ref,
                  seen_ref, ring_send, ring_recv, side_send, side_recv, load_sem, seen_sem):
    ring, z, core = place()
    loads = [pltpu.make_async_copy(src, dst, load_sem.at[n]) for n, (src, dst) in enumerate((
        (rule_hbm, rule_ref), (rw_hbm, rw_ref), (x_hbm, x_ref), (c_hbm, c_ref), (cols_hbm, cols_ref)))]
    for cp in loads:
        cp.start()
    barrier = pltpu.get_barrier_semaphore()
    peers = partners(ring, z, core)
    for peer in peers:
        pl.semaphore_signal(barrier, inc=1, device_id=peer, device_id_type=MESH)

    for cp in loads:
        cp.wait()
    rule = rule_ref[...]
    w = jnp.zeros((1, 512), jnp.float32)
    for r in range(RULES):
        w = jnp.where(rule == r, rw_ref[r], w)
    w_ref[...] = jnp.broadcast_to(w, (8, 512))
    b_ref[0:64, :] = x_ref[...] * (w * GAIN)
    b_ref[64:67, :] = c_ref[...] * WAVES
    b_ref[67:72, :] = jnp.full((5, 512), -2.0, jnp.float32)
    slot = lax.broadcasted_iota(jnp.int32, (1, SLOTS), 1)
    b_ref[67:68, 0:SLOTS] = jnp.where(slot < count_ref[0], cols_ref[...], -2).astype(jnp.float32)
    table_ref[...] = jnp.zeros_like(table_ref)

    pl.semaphore_wait(barrier, len(peers))
    started = []

    def launch(cp):
        cp.start()
        started.append(cp)

    def owner_of(way, h):
        return (z - (1 - 2 * way) * h) % RING_LEN

    def hop(way, h, ch):
        owner = owner_of(way, h)
        rows = pl.ds(CUTS[ch], CUTS[ch + 1] - CUTS[ch])
        src = b_ref.at[rows] if h == 0 else bi_ref.at[owner, rows]
        return remote(src, bi_ref.at[owner, rows], ring_send.at[way, h, ch], ring_recv.at[way, h, ch],
                      device(ring, z + 1 - 2 * way, core))

    order = [(way, c if way == 0 else NCH - 1 - c) for c in range(NCH) for way in range(2)]
    for way, ch in order:
        launch(hop(way, 0, ch))
    for n, (d, c) in enumerate(((1, 0), (1, 1), (2, 0), (2, 1))):
        launch(remote(b_ref, bj_ref.at[d * 2 + core], side_send.at[n],
                      side_recv.at[d * 2 + core], device(ring - d, z, c)))
    launch(remote(b_ref, bj_ref.at[core], side_send.at[4], side_recv.at[core],
                  device(ring, z, 1 - core)))

    lane = lax.broadcasted_iota(jnp.int32, (16, 128), 1)
    col = lax.broadcasted_iota(jnp.int32, (16, 128), 0)
    want = jnp.where(col < 12, (ring + col // 4) * 32 + z * 4 + col % 4, -1).astype(jnp.float32)

    def expand_i(src, k, listed=True):
        fill_vectors(src, k, li_ref)
        t = src[64:72, :].T
        for h in range(2):
            for d in range(3):
                p_ref[2 * k + h, d] = jnp.broadcast_to(t[h * BLOCK:(h + 1) * BLOCK, d:d + 1], (BLOCK, 128))
        if not listed:
            return
        hit = jnp.where(jnp.broadcast_to(src[67:68, 0:128], (16, 128)) == want, 1.0, 0.0)
        for i in range(2):
            m = jnp.sum(jnp.where(lane % 2 == i, hit, 0.0), axis=1, keepdims=True)
            table_ref[...] += jnp.where(lane == 2 * k + i, m, 0.0).astype(jnp.int32)

    def expand_j(src, k):
        fill_vectors(src, k, lj_ref)
        for h in range(2):
            q_ref[2 * k + h] = src[64:72, h * BLOCK:(h + 1) * BLOCK]

    expand_i(b_ref, z)
    expand_j(b_ref, core)
    for h in range(1, HOPS):
        for way, ch in order:
            hop(way, h - 1, ch).wait_recv()
            if h < HOPS - 1 or far(way, ch):
                launch(hop(way, h, ch))
        for way in range(2):
            k = owner_of(way, h)
            expand_i(bi_ref.at[k], k)
        js = ((1 - core, 4),) if h == 1 else ((4, 0), (5, 0)) if h == 2 else ((2, 0), (3, 0))
        for k, n in js:
            remote(b_ref, bj_ref.at[k], side_send.at[n], side_recv.at[k],
                   device(ring, z, 1 - core)).wait_recv()
            expand_j(bj_ref.at[k], k)
            if n == 4:
                expand_i(bj_ref.at[k], RING_LEN, listed=False)
        if h == HOPS - 1:
            have = table_ref[...]
            tally = jnp.sum(jnp.where(have > 0, 1.0, 0.0)).astype(jnp.int32)
            have = jnp.where(col == 15, tally, have)
            seen_ref[...] = have
            table_ref[...] = have
    note = remote(seen_ref, other_ref, seen_sem.at[0], seen_sem.at[1], device(ring, z, 1 - core))
    note.start()
    for way in range(2):
        for ch in range(NCH):
            if far(way, ch):
                hop(way, HOPS - 1, ch).wait_recv()
    k = (z + HOPS) % RING_LEN
    expand_i(bi_ref.at[k], k)
    note.wait()
    for cp in started:
        cp.wait_send()


def gather(x, coords, rule, rw, cols, count):
    f = jnp.float32
    b = jnp.bfloat16
    dma = pltpu.SemaphoreType.DMA
    s = jax.ShapeDtypeStruct
    return pl.pallas_call(
        gather_kernel,
        out_shape=(s((18, 128, 512), b), s((12, 128, 512), b), s((18, 3, 256, 128), f), s((12, 8, 256), f),
                   s((16, 128), jnp.int32), s((16, 128), jnp.int32), s((8, 512), f)),
        in_specs=[HBM] * 5 + [pl.BlockSpec(memory_space=pltpu.SMEM)],
        out_specs=(VM,) * 7,
        scratch_shapes=[pltpu.VMEM((PACK, 512), f), pltpu.VMEM((8, PACK, 512), f), pltpu.VMEM((6, PACK, 512), f),
                        pltpu.VMEM((64, 512), f), pltpu.VMEM((3, 512), f), pltpu.VMEM((1, 512), jnp.int32),
                        pltpu.VMEM((1, SLOTS), jnp.int32), pltpu.SMEM((RULES,), f), pltpu.VMEM((16, 128), jnp.int32),
                        dma((2, HOPS, NCH)), dma((2, HOPS, NCH)), dma((5,)), dma((6,)), dma((5,)), dma((2,))],
        compiler_params=pltpu.CompilerParams(collective_id=0, has_side_effects=True, vmem_limit_bytes=20 << 20),
    )(x, coords, rule, rw, cols, count)


def build_tile(row, col, p_ref, q_ref, hi_ref, lo_ref):
    qx = q_ref[col, 0:1, :]
    qy = q_ref[col, 1:2, :]
    qz = q_ref[col, 2:3, :]
    for r in range(0, BLOCK, ROWS):
        px = p_ref[row, 0, r:r + ROWS, :]
        py = p_ref[row, 1, r:r + ROWS, :]
        pz = p_ref[row, 2, r:r + ROWS, :]
        dx = jnp.concatenate([px, px], axis=1) - qx
        dy = jnp.concatenate([py, py], axis=1) - qy
        dz = jnp.concatenate([pz, pz], axis=1) - qz
        square = dx * dx + (dy * dy + (dz * dz + SMOOTH))
        inv = lax.rsqrt(square)
        turns = square * inv
        f = turns - jnp.round(turns)
        f2 = f * f
        poly = SINE[-1]
        for k in SINE[-2::-1]:
            poly = poly * f2 + k
        s = f * poly
        ss = s * s
        rest = FULL - ss
        sh = s * (rest * lax.rsqrt(rest))
        ch = HALF - ss
        t = inv * sh
        rh, rl = split(inv - t * sh)
        ih, il = split(t * ch)
        hi_ref[r:r + ROWS, 0:BLOCK] = rh
        hi_ref[r:r + ROWS, BLOCK:] = ih
        lo_ref[r:r + ROWS, 0:BLOCK] = rl
        lo_ref[r:r + ROWS, BLOCK:] = il


def dotf(a, b, dims):
    return lax.dot_general(a, b, dims, preferred_element_type=jnp.float32)


def apply_tile(row, col, md, mm, li_ref, lj_ref, hi_ref, lo_ref, yi_ref, yj_ref):
    a = dotf(lj_ref[col], hi_ref[...], NT)
    b = dotf(lj_ref[col, 0:64, :], lo_ref[...], NT)
    yi_ref[row] += md * (a[:64] + a[64:] + b)
    a = dotf(li_ref[row, :, 0:BLOCK], hi_ref[:, 0:BLOCK], NN) + dotf(li_ref[row, :, BLOCK:], hi_ref[:, BLOCK:], NN)
    b = dotf(li_ref[row, 0:64, 0:BLOCK], lo_ref[:, 0:BLOCK], NN) + dotf(
        li_ref[row, 0:64, BLOCK:], lo_ref[:, BLOCK:], NN)
    yj_ref[col] += mm * (a[:64] + a[64:] + b)


def compute_kernel(li, lj, p, q, table, other, yi_ref, yj_ref, counts, theirs, work, hi0, lo0, hi1, lo1, sem):
    _, z, core = place()
    loads = [pltpu.make_async_copy(table, counts, sem.at[0]), pltpu.make_async_copy(other, theirs, sem.at[1])]
    for cp in loads:
        cp.start()
    yi_ref[...] = jnp.zeros_like(yi_ref)
    yj_ref[...] = jnp.zeros_like(yj_ref)
    build_tile(2 * z, 2 * core, p, q, hi0, lo0)
    for cp in loads:
        cp.wait()

    gap = counts[15, 0] - theirs[15, 0]
    give = jnp.where(gap > 0, lax.shift_right_logical(gap, 1), 0)
    take = jnp.where(gap < 0, lax.shift_right_logical(-gap, 1), 0)

    def scan_own(ref, first, label, keep):
        def inner(n, passed):
            for i in range(2):
                for j in range(12):
                    m = ref[j, first + i]
                    work[n] = (label + i) * 4096 + j * 256 + m
                    live = m > 0
                    n = n + jnp.where(jnp.logical_and(live, keep(passed)), 1, 0)
                    passed = passed + jnp.where(live, 1, 0)
            return n
        return inner

    n = scan_own(counts, 2 * z, 2 * z, lambda k: jnp.logical_or(k == 0, k > give))(jnp.int32(0), jnp.int32(0))
    n = scan_own(theirs, 2 * z, 2 * RING_LEN, lambda k: jnp.logical_and(k > 0, k <= take))(n, jnp.int32(0))

    def scan_row(k, n):
        row = (2 * z + k) % (2 * RING_LEN)
        base = jnp.where(row > 2 * z, 4, 0)
        for j in range(8):
            m = counts[base + j, row]
            work[n] = row * 4096 + (base + j) * 256 + m
            n = n + jnp.where(m > 0, 1, 0)
        return n

    n = lax.fori_loop(2, 2 * RING_LEN, scan_row, n)
    for e in range(3):
        work[n + e] = 0

    def unpack(t):
        w = work[t]
        row = lax.shift_right_logical(w, 12)
        col = lax.shift_right_logical(w, 8) & 15
        m = w & 255
        owner = jnp.where(lax.shift_right_logical(row, 1) == RING_LEN, 1 - core, core)
        local = jnp.logical_or(lax.shift_right_logical(row, 1) == z, row >= 2 * RING_LEN)
        same = jnp.logical_and(local, col == owner * 2 + (row & 1))
        return row, col, m.astype(jnp.float32), jnp.where(same, 0, m).astype(jnp.float32)


    @pl.loop(0, n // 2)
    def _(k):
        r0, c0, d0, m0 = unpack(2 * k)
        r1, c1, d1, m1 = unpack(2 * k + 1)
        r2, c2, _, _ = unpack(2 * k + 2)
        build_tile(r1, c1, p, q, hi1, lo1)
        apply_tile(r0, c0, d0, m0, li, lj, hi0, lo0, yi_ref, yj_ref)
        build_tile(r2, c2, p, q, hi0, lo0)
        apply_tile(r1, c1, d1, m1, li, lj, hi1, lo1, yi_ref, yj_ref)

    @pl.when(n % 2 == 1)
    def _():
        row, col, md, mm = unpack(n - 1)
        apply_tile(row, col, md, mm, li, lj, hi0, lo0, yi_ref, yj_ref)

    for i in range(2):
        yj_ref[2 * (1 - core) + i] += yi_ref[2 * RING_LEN + i]


def compute(li, lj, p, q, table, other):
    f = jnp.float32
    b = jnp.bfloat16
    return pl.pallas_call(
        compute_kernel,
        out_shape=(jax.ShapeDtypeStruct((18, 64, 256), f), jax.ShapeDtypeStruct((12, 64, 256), f)),
        in_specs=[VM] * 6, out_specs=(VM, VM),
        scratch_shapes=[pltpu.SMEM((16, 128), jnp.int32), pltpu.SMEM((16, 128), jnp.int32),
                        pltpu.SMEM((256,), jnp.int32),
                        pltpu.VMEM((256, 512), b), pltpu.VMEM((256, 512), b),
                        pltpu.VMEM((256, 512), b), pltpu.VMEM((256, 512), b),
                        pltpu.SemaphoreType.DMA((2,))],
        compiler_params=pltpu.CompilerParams(vmem_limit_bytes=24 << 20),
    )(li, lj, p, q, table, other)


PARTS = 4
SPAN = 64 // PARTS


def near(way, ch):
    return ch // (PARTS // 2) == way


def reduce_kernel(yi_ref, yj_ref, w_ref, out_ref, flow, side, ring_send, ring_recv, side_send, side_recv):
    ring, z, core = place()
    barrier = pltpu.get_barrier_semaphore()
    peers = partners(ring, z, core)
    for peer in peers:
        pl.semaphore_signal(barrier, inc=1, device_id=peer, device_id_type=MESH)
    pl.semaphore_wait(barrier, len(peers))
    started = []

    def part(ref, first, ch):
        return ref.at[pl.ds(first, 2), pl.ds(SPAN * ch, SPAN)]

    def hop(way, h, ch, src):
        return remote(src, part(flow.at[way, h], 0, ch), ring_send.at[way, h, ch], ring_recv.at[way, h, ch],
                      device(ring, z + 1 - 2 * way, core))

    def target(way, h):
        return (z + (1 - 2 * way) * (HOPS - h)) % RING_LEN

    def launch(cp):
        cp.start()
        started.append(cp)

    for ch in range(PARTS):
        for way in range(2):
            if near(way, ch):
                launch(hop(way, 0, ch, part(yi_ref, 2 * target(way, 0), ch)))
    for ch in range(PARTS):
        for way in range(2):
            if not near(way, ch):
                launch(hop(way, 1, ch, part(yi_ref, 2 * target(way, 1), ch)))
    n = 0
    for d in (1, 2):
        for c in range(2):
            launch(remote(yj_ref.at[pl.ds((d * 2 + c) * 2, 2)], side.at[(d - 1) * 2 + core], side_send.at[n],
                          side_recv.at[(d - 1) * 2 + core], device(ring + d, z, c)))
            n += 1
    launch(remote(yj_ref.at[pl.ds((1 - core) * 2, 2)], side.at[4], side_send.at[4], side_recv.at[4],
                  device(ring, z, 1 - core)))
    for h in range(1, HOPS):
        for first in (False, True):
            for ch in range(PARTS):
                for way in range(2):
                    if near(way, ch) != first or (h == 1 and not first):
                        continue
                    here = part(flow.at[way, h - 1], 0, ch)
                    hop(way, h - 1, ch, here).wait_recv()
                    rows = slice(SPAN * ch, SPAN * ch + SPAN)
                    flow[way, h - 1, :, rows, :] += yi_ref[pl.ds(2 * target(way, h), 2), rows, :]
                    launch(hop(way, h, ch, here))
    for s in range(5):
        remote(side.at[s], side.at[s], side_send.at[s], side_recv.at[s], device(ring, z, 1 - core)).wait_recv()
    for h in range(2):
        total = yi_ref[2 * z + h] + yj_ref[2 * core + h]
        total += side[0, h] + side[1, h] + (side[2, h] + side[3, h]) + side[4, h]
        out_ref[:, h * BLOCK:(h + 1) * BLOCK] = total
    for way in range(2):
        for ch in range(PARTS):
            hop(way, HOPS - 1, ch, part(flow.at[way, 0], 0, ch)).wait_recv()
    for h in range(2):
        cols = slice(h * BLOCK, (h + 1) * BLOCK)
        total = out_ref[:, cols] + (flow[0, HOPS - 1, h] + flow[1, HOPS - 1, h])
        out_ref[:, cols] = total * w_ref[0:1, cols]
    for cp in started:
        cp.wait_send()


def reduce(yi, yj, w):
    f = jnp.float32
    dma = pltpu.SemaphoreType.DMA
    return pl.pallas_call(
        reduce_kernel,
        out_shape=jax.ShapeDtypeStruct((64, 512), f),
        in_specs=[VM] * 3, out_specs=VM,
        scratch_shapes=[pltpu.VMEM((2, HOPS, 2, 64, 256), f), pltpu.VMEM((5, 2, 64, 256), f),
                        dma((2, HOPS, PARTS)), dma((2, HOPS, PARTS)), dma((5,)), dma((5,))],
        compiler_params=pltpu.CompilerParams(collective_id=1, has_side_effects=True, vmem_limit_bytes=16 << 20),
    )(yi, yj, w)


def body(drive, coords, rule_index, rule_weight, pair_cols, pair_count):
    held = [pltpu.with_memory_space_constraint(v, pltpu.HBM) for v in (
        drive.reshape(64, 512), coords, rule_index.reshape(1, 512), rule_weight, pair_cols.reshape(1, SLOTS))]
    li, lj, p, q, table, other, w = gather(*held, pair_count)
    yi, yj = compute(li, lj, p, q, table, other)
    return reduce(yi, yj, w).reshape(2, 32, 512)


def solution(mesh):
    both = ("band", "dev")
    in_specs = (P(None, None, both), P(None, both), P(both), P(), P(both), P(both))
    return jax.shard_map(body, mesh=mesh, in_specs=in_specs, out_specs=P(None, None, both), check_vma=False)
```
